128 devices in a mesh: dp: 16 (over z, x), expert: 8 (over y, core).
Axes of the slice: x: 4, y: 4, z: 4, core: 2. Of those that a mesh axis runs over, the one named last changes fastest.
Arguments:
- tokens: bfloat16 [16384, 1280], P(('dp', 'expert')), may hold values from -6 to 6
- routes: int32 [16384, 2], P(('dp', 'expert')), may hold values from 0 to 31, all different within a row; in each aligned block of 128 rows (0 to 127, 128 to 255, ...) at most 10 rows name the same one
- combine: float32 [16384, 2], P(('dp', 'expert')), may hold values from 0.1 to 1
- w_in: bfloat16 [1280, 163840], P(None, ('dp', 'expert')), may hold values from -0.15625 to 0.15625
- w_out: bfloat16 [163840, 1280], P(('dp', 'expert')), may hold values from -0.078125 to 0.078125
- out_grad: bfloat16 [16384, 1280], P(('dp', 'expert')), may hold values from -6 to 6
- head_w: bfloat16 [1280, 17408], P(None, 'expert'), may hold values from -0.5 to 0.5
- labels: int32 [64, 4], P('dp'), may hold values from 0 to 17407
Outputs:
- mixed_out: bfloat16 [16384, 1280], P(('dp', 'expert'))
- d_tokens: bfloat16 [16384, 1280], P(('dp', 'expert'))
- d_combine: float32 [16384, 2], P(('dp', 'expert'))
- d_w_in: bfloat16 [1280, 163840], P(None, ('dp', 'expert'))
- d_w_out: bfloat16 [163840, 1280], P(('dp', 'expert'))
- image_loss: float32 [64], P('dp')
- d_pooled: float32 [64, 1280], P('dp')
- d_head: bfloat16 [1280, 17408], P('dp', 'expert')
The draws below stay inside these ranges and needn't reach their ends.
Inputs may be any that keep to these rules, and one draw needn't show every extreme that they name: `routes`: in the 128 rows of each device no expert is named by more than 10 rows, a bound that some block reaches; the two entries of a row differ. `labels`: entries of one image may repeat.
All inputs are finite; a program needn't handle non-finite values.
Results may differ from the reference program's by a relative error of at most 0.015.
Values may be sent and summed in bfloat16 or wider, within the bound.
No kernel may reach another device: no remote copies, remote signals or barrier semaphores. Data moves between devices by JAX's collectives and lax.ppermute only.
A program may use at most 192 MiB of HBM per device.

```python
import math
import jax
import jax.numpy as jnp
import numpy as np
from jax import lax

D = 1280
FF = 5120
EXPERTS = 32
PATCHES = 256
CLASSES = 17408
LAB = 4
TOK_DEV = 128
CAP = 10
TOKENS = 16384
IMAGES = 64
N_DP = 16
N_EXPERT = 8


def with_ends(array, key, low, top_value):
    dims = array.shape
    index_at = [jax.random.randint(jax.random.fold_in(key, axis), (), 0, dims[axis]) for axis in range(len(dims))]
    array = array.at[tuple(index_at)].set(low)
    longest = dims.index(max(dims))
    index_at[longest] = (index_at[longest] + 1) % dims[longest]
    return array.at[tuple(index_at)].set(top_value)


def steps_of(own_key, dims, pieces, low, top_value):
    def one(dim, blocks):
        heights = jax.random.uniform(jax.random.fold_in(jax.random.fold_in(own_key, 6), dim), (blocks,), jnp.float32, low / len(pieces), top_value / len(pieces))
        return jnp.repeat(jnp.exp(heights), dims[dim] // blocks).reshape((-1,) + (1,) * (len(dims) - dim - 1))

    loudness = one(*pieces[0])
    for cut in pieces[1:]:
        loudness = loudness * one(*cut)
    return loudness


def rank_table(count, skew):
    loads = [(1 << 20) // math.isqrt(standing ** skew) + 1 for standing in range(1, count + 1)]
    deviation = 1 + sum(loads) // (1 << 30)
    return np.cumsum(np.array([max(1, weight // deviation) for weight in loads]))


def ranked_ids(own_key, extent, count, skew):
    listing = rank_table(count, skew)
    lot = jax.random.randint(jax.random.fold_in(own_key, 1), extent, 0, int(listing[count - 1]))
    rank = jnp.searchsorted(jnp.asarray(listing, jnp.int32), lot, side="right")
    return jax.random.permutation(jax.random.fold_in(own_key, 2), count)[rank].astype(jnp.int32)


def routed_block(stream_key, own, number, rows, count, top, reach, slope):
    order = jax.random.permutation(stream_key, count)
    heavy_load, common = portions_of(count, rows * top, reach, slope, True), portions_of(count, rows * top, reach, slope, False)
    places = jnp.arange(count)

    def named(tallies, rotation):
        used = int((tallies > 0).sum())
        fixed = max(1, used // 4)
        shifted = fixed + (places - fixed + rotation * (used - fixed)) % max(1, count - fixed)
        return jnp.zeros((count,), jnp.int32).at[order[jnp.where(places < fixed, places, shifted)]].set(jnp.asarray(tallies, jnp.int32))

    tallies = jnp.where(number % 4 == 0, named(heavy_load, number // 4), named(common, number - number // 4 - 1))
    mixed = jax.random.permutation(jax.random.fold_in(own, 3), count)
    giver, sink = mixed[0:count // 2 * 2:2], mixed[1:count // 2 * 2:2]
    room = jnp.minimum(tallies[giver] - 1, reach - tallies[sink]) // 2
    room = jnp.where((giver == order[0]) | (sink == order[0]) | (tallies[sink] == 0), 0, jnp.maximum(room, 0))
    shifted = jax.random.randint(jax.random.fold_in(own, 4), (count // 2,), 0, 1 << 20) % (room + 1)
    tallies = tallies.at[giver].add(-shifted).at[sink].add(shifted)
    items = jnp.searchsorted(jnp.cumsum(tallies), jnp.arange(rows * top), side="right").astype(jnp.int32)
    grid = items.reshape(top, rows).T
    grid = grid[jax.random.permutation(jax.random.fold_in(own, 1), rows)]
    rotation = jax.random.randint(jax.random.fold_in(own, 2), (rows, 1), 0, top)
    return jnp.take_along_axis(grid, (jnp.arange(top)[None, :] + rotation) % top, axis=1)


def portions_of(amount, total, reach, lean, full):
    weights = [(1 << 20) // math.isqrt(standing ** lean) + 1 for standing in range(1, amount + 1)]
    largest = reach if full else min(reach, max(-(-total // amount), total * weights[0] // sum(weights)))
    least = 1 if total - largest >= amount - 1 else 0
    given, spare = [largest] + [least] * (amount - 1), total - largest - least * (amount - 1)
    while spare > 0:
        movable = [i for i in range(1, amount) if given[i] < largest] or [i for i in range(1, amount) if given[i] < reach]
        pool, left = sum([weights[i] for i in movable]), spare
        for i in movable:
            more = min(reach - given[i], max(1, left * weights[i] // pool), spare)
            given[i] = given[i] + more
            spare = spare - more
    return np.array(given)


def gaussian(key, dims, scale, reach, split=(), held_as=jnp.bfloat16):
    result = scale * jax.random.normal(key, dims, jnp.float32)
    if split:
        result = result * steps_of(key, dims, split, -0.22, 0.18)
    return jnp.clip(result, -reach, reach).astype(held_as)


def setup_inputs(seed: int = 0) -> dict:
    arg_keys = jax.random.split(jax.random.key(seed), 9)
    tokens = gaussian(arg_keys[0], (TOKENS, D), 1.0, 6.0, ((0, 128),))
    routes_keys = jax.random.split(jax.random.fold_in(arg_keys[1], 1), TOKENS // TOK_DEV)
    routes_turns = jax.random.permutation(jax.random.fold_in(arg_keys[1], 3), TOKENS // TOK_DEV)
    routes = jax.vmap(lambda own, number: routed_block(jax.random.fold_in(arg_keys[1], 2), own, number, TOK_DEV, EXPERTS, 2, CAP, 2))(routes_keys, routes_turns).reshape((TOKENS, 2))
    combine = jnp.clip(jnp.exp(math.log(1.0) - 2.3025851 * jax.random.uniform(arg_keys[2], (TOKENS, 2), jnp.float32) ** steps_of(arg_keys[2], (TOKENS, 2), ((0, 128),), -0.2, 0.2)), 0.1, 1.0)
    w_in = gaussian(arg_keys[3], (D, EXPERTS * FF), D ** -0.5, 0.15625, ((1, 128),))
    w_out = gaussian(arg_keys[4], (EXPERTS * FF, D), FF ** -0.5, 0.078125, ((0, 128),))
    out_grad = gaussian(arg_keys[5], (TOKENS, D), 1.0, 6.0, ((0, 128),))
    head_w = gaussian(arg_keys[6], (D, CLASSES), (D // 9) ** -0.5, 0.5, ((1, 8),))
    labels = with_ends(ranked_ids(arg_keys[7], (IMAGES, LAB), CLASSES, 2), jax.random.fold_in(arg_keys[7], 3), 0, CLASSES - 1).astype(jnp.int32)
    return {"tokens": tokens, "routes": routes, "combine": combine, "w_in": w_in, "w_out": w_out, "out_grad": out_grad, "head_w": head_w, "labels": labels}


beta_rate = 0.99
norm_eps = 1e-06

def gelu_fn(values):
    return jax.nn.gelu(values, approximate=True)

def normalize(pooled):
    center = lax.optimization_barrier(jnp.mean(pooled, axis=1, keepdims=True))
    spread = lax.optimization_barrier(jnp.mean(jnp.square(pooled - center), axis=1, keepdims=True))
    return (pooled - center) * lax.rsqrt(spread + norm_eps)

def weighted_focal(logit_vals, targets, class_weight):
    nll_vals = targets * jax.nn.softplus(-logit_vals) + (1.0 - targets) * jax.nn.softplus(logit_vals)
    return class_weight[None, :] * jnp.square(1.0 - jnp.exp(-nll_vals)) * nll_vals

def expert_pass(xs_rows, grad_rows, w_first, w_second):
    h_pre = jnp.dot(xs_rows, w_first, preferred_element_type=jnp.float32)
    hidden, gelu_back = jax.vjp(gelu_fn, h_pre)
    hidden_bf = hidden.astype(jnp.bfloat16)
    expert_out = jnp.dot(hidden_bf, w_second, preferred_element_type=jnp.float32)
    d_hidden = lax.dot_general(grad_rows, w_second, (((1,), (1,)), ((), ())), preferred_element_type=jnp.float32)
    d_pre = gelu_back(d_hidden)[0].astype(jnp.bfloat16)
    d_second = lax.dot_general(hidden_bf, grad_rows, (((0,), (0,)), ((), ())), preferred_element_type=jnp.float32).astype(jnp.bfloat16)
    d_first = lax.dot_general(xs_rows, d_pre, (((0,), (0,)), ((), ())), preferred_element_type=jnp.float32).astype(jnp.bfloat16)
    d_rows = lax.dot_general(d_pre, w_first, (((1,), (1,)), ((), ())), preferred_element_type=jnp.float32)
    return (expert_out, d_rows, d_first, d_second)

def reference(tokens, routes, combine, w_in, w_out, out_grad, head_w, labels):
    n_devices = N_DP * N_EXPERT
    flat_routes = routes.reshape(n_devices, TOK_DEV * 2)
    route_hits = (flat_routes[:, :, None] == jnp.arange(EXPERTS, dtype=jnp.int32)[None, None, :]).astype(jnp.int32)
    earlier = jnp.cumsum(route_hits, axis=1) - route_hits
    slot_pos = lax.optimization_barrier(jnp.sum(earlier * route_hits, axis=2)).astype(jnp.int32)
    dev_ids = jnp.broadcast_to(jnp.arange(n_devices, dtype=jnp.int32)[:, None], flat_routes.shape)
    tok_pairs = jnp.broadcast_to(tokens.reshape(n_devices, TOK_DEV, 1, D), (n_devices, TOK_DEV, 2, D)).reshape(n_devices, TOK_DEV * 2, D)
    pair_grad = (combine[:, :, None] * out_grad.astype(jnp.float32)[:, None, :]).astype(jnp.bfloat16)
    grad_pairs = pair_grad.reshape(n_devices, TOK_DEV * 2, D)
    x_buf = jnp.zeros((EXPERTS, n_devices, CAP, D), jnp.bfloat16).at[flat_routes, dev_ids, slot_pos].set(tok_pairs)
    g_buf = jnp.zeros((EXPERTS, n_devices, CAP, D), jnp.bfloat16).at[flat_routes, dev_ids, slot_pos].set(grad_pairs)
    w_in_e = w_in.reshape(D, EXPERTS, FF).transpose(1, 0, 2)
    w_out_e = w_out.reshape(EXPERTS, FF, D)

    def one_expert(operands):
        xs_block, grad_block, w_first, w_second = operands
        return expert_pass(xs_block.reshape(n_devices * CAP, D), grad_block.reshape(n_devices * CAP, D), w_first, w_second)
    outs_e, drows_e, dfirst_e, dsecond_e = lax.map(one_expert, (x_buf, g_buf, w_in_e, w_out_e))
    expert_vals = outs_e.reshape(EXPERTS, n_devices, CAP, D)[flat_routes, dev_ids, slot_pos].reshape(TOKENS, 2, D)
    expert_back = drows_e.reshape(EXPERTS, n_devices, CAP, D)[flat_routes, dev_ids, slot_pos].reshape(TOKENS, 2, D)
    mixed_out = (tokens.astype(jnp.float32) + lax.optimization_barrier(jnp.sum(combine[:, :, None] * expert_vals, axis=1))).astype(jnp.bfloat16)
    d_tokens = (out_grad.astype(jnp.float32) + lax.optimization_barrier(jnp.sum(expert_back, axis=1))).astype(jnp.bfloat16)
    d_combine = lax.optimization_barrier(jnp.sum(out_grad.astype(jnp.float32)[:, None, :] * expert_vals, axis=2))
    d_w_in = dfirst_e.transpose(1, 0, 2).reshape(D, EXPERTS * FF)
    d_w_out = dsecond_e.reshape(EXPERTS * FF, D)
    pooled = lax.optimization_barrier(jnp.sum(mixed_out.astype(jnp.float32).reshape(IMAGES, PATCHES, D), axis=1)) / PATCHES
    normed, norm_back = jax.vjp(normalize, pooled)
    normed_bf = normed.astype(jnp.bfloat16)
    logits = jnp.dot(normed_bf, head_w, preferred_element_type=jnp.float32)
    class_ids = jnp.arange(CLASSES, dtype=jnp.int32)
    targets = jnp.any(labels[:, :, None] == class_ids[None, None, :], axis=1).astype(jnp.float32)
    counts = lax.optimization_barrier(jnp.sum(targets, axis=0))
    effective = (1.0 - beta_rate) / (1.0 - jnp.power(beta_rate, counts + 1.0))
    class_weight = effective * CLASSES / jnp.sum(effective)
    focal_terms, focal_back = jax.vjp(lambda logit_vals: weighted_focal(logit_vals, targets, class_weight), logits)
    image_loss = lax.optimization_barrier(jnp.sum(focal_terms, axis=1))
    d_logits = focal_back(jnp.ones_like(focal_terms))[0].astype(jnp.bfloat16)
    d_head = lax.dot_general(normed_bf, d_logits, (((0,), (0,)), ((), ())), preferred_element_type=jnp.float32).astype(jnp.bfloat16)
    d_normed = lax.dot_general(d_logits, head_w, (((1,), (1,)), ((), ())), preferred_element_type=jnp.float32)
    d_pooled = norm_back(d_normed)[0]
    return (mixed_out, d_tokens, d_combine, d_w_in, d_w_out, image_loss, d_pooled, d_head)
```

```python
import jax
import jax.numpy as jnp
from jax import lax
from jax.sharding import Mesh, PartitionSpec as P

D = 1280
EXPERTS = 32
PATCHES = 256
CLASSES = 17408
CAP = 10
CHIPS = 64
IMAGES = 64
BETA = 0.99
EPS = 1e-06

CHIP = ("dp", "yh", "yl")
EX = ("yh", "yl", "core")
ALL = ("dp", "yh", "yl", "core")
SWAP = [(0, 1), (1, 0)]
F32 = jnp.float32
BF16 = jnp.bfloat16


def dot(a, b, ca, cb):
    return lax.dot_general(a, b, (((ca,), (cb,)), ((), ())), preferred_element_type=F32)


def chip_swap(rows):
    packed = rows.reshape(CHIPS, CAP // 2, 2, D)
    return lax.all_to_all(packed, CHIP, 0, 0, tiled=True).reshape(CHIPS * CAP, D)


def both_cores(rows):
    return jnp.concatenate([rows, lax.ppermute(rows, "core", SWAP)], axis=0)


def reduce_cores(partial):
    half = CHIPS * CAP
    other = lax.ppermute(partial[half:].astype(BF16), "core", SWAP)
    return (partial[:half] + other.astype(F32)).astype(BF16)


def gelu_fn(values):
    return jax.nn.gelu(values, approximate=True)


def normalize(pooled):
    center = jnp.mean(pooled, axis=1, keepdims=True)
    spread = jnp.mean(jnp.square(pooled - center), axis=1, keepdims=True)
    return (pooled - center) * lax.rsqrt(spread + EPS)


def weighted_focal(logit_vals, targets, class_weight):
    nll_vals = targets * jax.nn.softplus(-logit_vals) + (1.0 - targets) * jax.nn.softplus(
        logit_vals
    )
    return class_weight[None, :] * jnp.square(1.0 - jnp.exp(-nll_vals)) * nll_vals


def effective_of(counts):
    return (1.0 - BETA) / (1.0 - jnp.power(BETA, counts + 1.0))


def shards(tokens, routes, combine, w_in, w_out, out_grad, head_w, labels):
    tok = tokens.shape[0]
    dp_index = lax.axis_index("dp")
    ex_index = lax.axis_index(EX)
    expert_ids = jnp.arange(EXPERTS, dtype=jnp.int32)
    hit0 = routes[:, 0:1] == expert_ids[None, :]
    hit1 = routes[:, 1:2] == expert_ids[None, :]
    t_ids = jnp.arange(tok, dtype=jnp.int32)
    before = (t_ids[:, None] > t_ids[None, :]).astype(BF16)
    earlier = dot(before, (hit0 | hit1).astype(BF16), 1, 0).astype(jnp.int32)
    pos0 = jnp.sum(jnp.where(hit0, earlier, 0), axis=1)
    pos1 = jnp.sum(jnp.where(hit1, earlier, 0), axis=1)
    row0 = routes[:, 0] * (2 * CAP) + pos0
    row1 = routes[:, 1] * (2 * CAP) + pos1
    row = jnp.concatenate([row0, row1])
    r_ids = jnp.arange(CHIPS * CAP, dtype=jnp.int32)
    base = r_ids - CAP * ((r_ids // CAP) % 2)
    table = (base[:, None] == row[None, :]).astype(BF16)
    x_send = dot(table[:, :tok] + table[:, tok:], tokens, 1, 0).astype(BF16)
    grad_f = out_grad.astype(F32)
    pair_grad = jnp.concatenate(
        [(combine[:, 0:1] * grad_f).astype(BF16), (combine[:, 1:2] * grad_f).astype(BF16)], axis=0
    )
    g_send = dot(table, pair_grad, 1, 0).astype(BF16)
    xs = both_cores(chip_swap(x_send))
    gs = both_cores(chip_swap(g_send))
    h_pre = dot(xs, w_in, 1, 0)
    hidden, gelu_back = jax.vjp(gelu_fn, h_pre)
    hidden = hidden.astype(BF16)
    back_out = chip_swap(reduce_cores(dot(hidden, w_out, 1, 0)))
    d_pre = gelu_back(dot(gs, w_out, 1, 1))[0].astype(BF16)
    back_rows = chip_swap(reduce_cores(dot(d_pre, w_in, 1, 1)))
    d_w_out = dot(hidden, gs, 0, 0).astype(BF16)
    d_w_in = dot(xs, d_pre, 0, 0).astype(BF16)
    vals = dot(table, back_out, 0, 0)
    vals0, vals1 = vals[:tok], vals[tok:]
    mixed_out = (
        tokens.astype(F32) + (combine[:, 0:1] * vals0 + combine[:, 1:2] * vals1)
    ).astype(BF16)
    d_combine = jnp.stack(
        [jnp.sum(grad_f * vals0, axis=1), jnp.sum(grad_f * vals1, axis=1)], axis=1
    )
    backs = dot(table, back_rows, 0, 0)
    d_tokens = (grad_f + (backs[:tok] + backs[tok:])).astype(BF16)
    pooled_own = lax.psum(jnp.sum(mixed_out.astype(F32), axis=0), "core") / PATCHES
    spread_out = jnp.broadcast_to(pooled_own.reshape(1, 10, 128), (CHIPS, 10, 128))
    pooled = lax.all_to_all(spread_out, CHIP, 0, 0, tiled=True).reshape(IMAGES, D)
    own_labels = jnp.broadcast_to(labels.reshape(1, 16), (16, 16))
    all_labels = lax.all_to_all(own_labels, "dp", 0, 0, tiled=True).reshape(IMAGES, 4)
    flat = all_labels.reshape(IMAGES * 4)
    entry = jnp.arange(IMAGES * 4, dtype=jnp.int32)
    same = flat[:, None] == flat[None, :]
    sooner = entry[:, None] > entry[None, :]
    same_image = (entry[:, None] // 4) == (entry[None, :] // 4)
    fresh = ~jnp.any(same & sooner & same_image, axis=1)
    first = ~jnp.any(same & sooner, axis=1)
    entry_count = jnp.sum((same & fresh[None, :]).astype(F32), axis=1)
    distinct = jnp.sum(first.astype(F32))
    effective_total = (CLASSES - distinct) * effective_of(jnp.zeros((), F32)) + jnp.sum(
        jnp.where(first, effective_of(entry_count), 0.0)
    )
    class_cols = head_w.shape[1]
    class_ids = ex_index * class_cols + jnp.arange(class_cols, dtype=jnp.int32)
    targets = jnp.any(all_labels[:, :, None] == class_ids[None, None, :], axis=1).astype(F32)
    class_weight = effective_of(jnp.sum(targets, axis=0)) * CLASSES / effective_total
    normed_bf = normalize(pooled).astype(BF16)
    logits = dot(normed_bf, head_w, 1, 0)
    focal_terms, focal_back = jax.vjp(
        lambda logit_vals: weighted_focal(logit_vals, targets, class_weight), logits
    )
    d_logits = focal_back(jnp.ones_like(focal_terms))[0].astype(BF16)
    own_logits = lax.dynamic_slice_in_dim(d_logits, dp_index * 4, 4, 0)
    own_loss = jnp.sum(lax.dynamic_slice_in_dim(focal_terms, dp_index * 4, 4, 0), axis=1)
    normed_part = dot(own_logits, head_w, 1, 1)
    message = jnp.concatenate(
        [normed_part.reshape(40, 128), jnp.broadcast_to(own_loss[:, None], (4, 128)), jnp.zeros((4, 128), F32)], axis=0
    )
    parts = lax.all_to_all(
        jnp.broadcast_to(message[None], (8, 48, 128)), EX, 0, 0, tiled=True
    )
    total = jnp.sum(parts, axis=0)
    d_normed = total[:40].reshape(4, D)
    image_loss = total[40:44, 0]
    own_pooled = lax.dynamic_slice_in_dim(pooled, dp_index * 4, 4, 0)
    _, norm_back = jax.vjp(normalize, own_pooled)
    d_pooled = norm_back(d_normed)[0]
    own_cols = lax.dynamic_slice_in_dim(normed_bf, dp_index * 80, 80, 1)
    d_head = dot(own_cols, d_logits, 0, 0).astype(BF16)
    return (mixed_out, d_tokens, d_combine, d_w_in, d_w_out, image_loss, d_pooled, d_head)


def solution(mesh):
    grid = Mesh(mesh.devices.reshape(16, 2, 2, 2), ALL)
    rows = P(ALL, None)
    in_specs = (rows, rows, rows, P(None, ALL), rows, rows, P(None, EX), P("dp", None))
    out_specs = (
        rows,
        rows,
        rows,
        P(None, ALL),
        rows,
        P("dp"),
        P("dp", None),
        P("dp", EX),
    )
    return jax.shard_map(shards, mesh=grid, in_specs=in_specs, out_specs=out_specs, check_vma=False)
```

```python
import jax
import jax.numpy as jnp
from jax import lax
from jax.experimental import pallas as pl
from jax.experimental.pallas import tpu as pltpu
from jax.sharding import Mesh, PartitionSpec as P

D = 1280
EXPERTS = 32
PATCHES = 256
CLASSES = 17408
CAP = 10
CHIPS = 64
IMAGES = 64
TOK = 128
HALF = CHIPS * CAP
ROWS = 2 * HALF
COLS = CLASSES // 8
BETA = 0.99
EPS = 1e-06

CHIP = ("dp", "yh", "yl")
Y = ("yh", "yl")
EX = ("yh", "yl", "core")
ALL = ("dp", "yh", "yl", "core")
SWAP = [(0, 1), (1, 0)]
F32 = jnp.float32
BF16 = jnp.bfloat16
I32 = jnp.int32
PACKED = (HALF // 2, 2, D)
ROOT_2_PI = 0.7978845608028654
CUBIC = 0.044715


def dot(a, b, ca, cb):
    return lax.dot_general(a, b, (((ca,), (cb,)), ((), ())), preferred_element_type=F32)


def shape(dims, dtype):
    return jax.ShapeDtypeStruct(dims, dtype)


VMEM = pl.BlockSpec(memory_space=pltpu.VMEM)
SMEM = pl.BlockSpec(memory_space=pltpu.SMEM)
ANY = pl.BlockSpec(memory_space=pl.ANY)


TINY = pl.CostEstimate(flops=1, transcendentals=0, bytes_accessed=1)


def run(body, outs, *args, specs=None, scratch=(), name=None):
    return pl.pallas_call(
        body,
        out_shape=outs,
        in_specs=specs or [VMEM] * len(args),
        out_specs=jax.tree.map(lambda _: VMEM, outs),
        scratch_shapes=list(scratch),
        name=name,
        cost_estimate=TINY,
        compiler_params=pltpu.CompilerParams(vmem_limit_bytes=56 << 20),
    )(*args)


def pack_rows(ref, value):
    ref[...] = value.astype(BF16).reshape(PACKED)


def x_body(routes_ref, tokens_ref, table_ref, send_ref):
    ids = lax.broadcasted_iota(I32, (TOK, EXPERTS), 1)
    r0, r1 = routes_ref[:, 0:1], routes_ref[:, 1:2]
    hit0, hit1 = r0 == ids, r1 == ids
    hits = jnp.where(hit0, 1.0, jnp.where(hit1, 1.0, 0.0)).astype(BF16)
    t_row = lax.broadcasted_iota(I32, (TOK, TOK), 0)
    t_col = lax.broadcasted_iota(I32, (TOK, TOK), 1)
    before = jnp.where(t_row > t_col, 1.0, 0.0).astype(BF16)
    earlier = dot(before, hits, 1, 0)
    col = lax.broadcasted_iota(I32, (TOK, HALF), 1)
    both = jnp.zeros((TOK, HALF), F32)
    for k, (route, hit) in enumerate(((r0, hit0), (r1, hit1))):
        pos = jnp.sum(jnp.where(hit, earlier, 0.0), axis=1, keepdims=True)
        row = route * (2 * CAP) + pos.astype(I32)
        table = jnp.where(col == row, 1.0, jnp.where(col == row + CAP, 1.0, 0.0))
        table_ref[k] = table.astype(BF16)
        both = both + table
    pack_rows(send_ref, dot(both.astype(BF16), tokens_ref[...], 0, 0))


def g_body(table_ref, grad_ref, combine_ref, send_ref):
    grad = grad_ref[...].astype(F32)
    rows = dot(table_ref[0], (combine_ref[:, 0:1] * grad).astype(BF16), 0, 0)
    rows = rows + dot(table_ref[1], (combine_ref[:, 1:2] * grad).astype(BF16), 0, 0)
    pack_rows(send_ref, rows)


CHUNK = 320


def fetch(pairs, sems):
    copies = [pltpu.make_async_copy(s, d, sems.at[i]) for i, (s, d) in enumerate(pairs)]
    for copy in copies:
        copy.start()
    return copies


def forward_body(x_own, x_other, w1_hbm, w2_hbm, xs, hidden, slope, own, other, w1, w2, sems):
    first, second = fetch(((w1_hbm, w1), (w2_hbm, w2)), sems)
    xs[:HALF] = x_own[...].reshape(HALF, D)
    xs[HALF:] = x_other[...].reshape(HALF, D)
    first.wait()
    second.wait()

    def step(i, carry):
        for base in (0, HALF):
            rows = pl.ds(pl.multiple_of(base + i * CHUNK, CHUNK), CHUNK)
            h = dot(xs[rows, :], w1[...], 1, 0)
            square = h * h
            bend = jnp.tanh(ROOT_2_PI * h * (1.0 + CUBIC * square))
            half = 0.5 * (1.0 + bend)
            act = (h * half).astype(BF16)
            hidden[rows, :] = act
            slope[rows, :] = (
                half
                + 0.5 * h * (1.0 - bend * bend) * (ROOT_2_PI * (1.0 + 3.0 * CUBIC * square))
            ).astype(BF16)
            part = dot(act, w2[...], 1, 0)
            out_rows = pl.ds(pl.multiple_of(i * CHUNK, CHUNK), CHUNK)
            if base == 0:
                own[out_rows, :] = part
            else:
                other[out_rows, :] = part.astype(BF16)
        return carry

    lax.fori_loop(0, HALF // CHUNK, step, 0)


def backward_body(g_own, g_other, slope, w1_hbm, w2_hbm, gs, d_pre, own, other, w1, w2, sems):
    second, first = fetch(((w2_hbm, w2), (w1_hbm, w1)), sems)
    gs[:HALF] = g_own[...].reshape(HALF, D)
    gs[HALF:] = g_other[...].reshape(HALF, D)
    second.wait()
    first.wait()

    def step(i, carry):
        for base in (0, HALF):
            rows = pl.ds(pl.multiple_of(base + i * CHUNK, CHUNK), CHUNK)
            d_h = dot(gs[rows, :], w2[...], 1, 1)
            act = (d_h * slope[rows, :].astype(F32)).astype(BF16)
            d_pre[rows, :] = act
            part = dot(act, w1[...], 1, 1)
            out_rows = pl.ds(pl.multiple_of(i * CHUNK, CHUNK), CHUNK)
            if base == 0:
                own[out_rows, :] = part
            else:
                other[out_rows, :] = part.astype(BF16)
        return carry

    lax.fori_loop(0, HALF // CHUNK, step, 0)


WEIGHTS = (
    pltpu.VMEM((D, D), BF16),
    pltpu.VMEM((D, D), BF16),
    pltpu.SemaphoreType.DMA((2,)),
)
SQUARE = (ROWS, D)


def add_body(own_ref, other_ref, send_ref):
    pack_rows(send_ref, own_ref[...] + other_ref[...].astype(F32))


def add_cores(own, other, name):
    there = lax.ppermute(other, "core", SWAP)
    return run(add_body, shape(PACKED, BF16), own, there, name=name)


def mixed_body(table_ref, in_ref, tokens_ref, grad_ref, combine_ref, mixed_ref, dc_ref, sum_ref):
    rows = in_ref[...].reshape(HALF, D)
    vals0 = dot(table_ref[0], rows, 1, 0)
    vals1 = dot(table_ref[1], rows, 1, 0)
    grad = grad_ref[...].astype(F32)
    dc_ref[:, 0:1] = jnp.sum(grad * vals0, axis=1, keepdims=True)
    dc_ref[:, 1:2] = jnp.sum(grad * vals1, axis=1, keepdims=True)
    mixed = (
        tokens_ref[...].astype(F32)
        + (combine_ref[:, 0:1] * vals0 + combine_ref[:, 1:2] * vals1)
    ).astype(BF16)
    mixed_ref[...] = mixed
    sum_ref[...] = jnp.sum(mixed.astype(F32), axis=0, keepdims=True)


def tokens_body(table_ref, in_ref, grad_ref, out_ref):
    rows = in_ref[...].reshape(HALF, D)
    table = table_ref[0].astype(F32) + table_ref[1].astype(F32)
    out_ref[...] = (grad_ref[...].astype(F32) + dot(table.astype(BF16), rows, 1, 0)).astype(BF16)


def in_order(here, parts, j):
    pick = parts[0]
    for shift in (1, 2, 3):
        pick = jnp.where((here + shift) % 4 == j, parts[shift], pick)
    return pick


def y_parts(mine):
    return [mine] + [
        lax.ppermute(mine, Y, [((i + shift) % 4, i) for i in range(4)]) for shift in (1, 2, 3)
    ]


def dp_gather(mine):
    for step in (1, 2, 4, 8):
        there = lax.ppermute(mine, "dp", [((i + step) % 16, i) for i in range(16)])
        mine = jnp.concatenate([mine, there], axis=0)
    return mine


def centered(pooled):
    away = pooled - jnp.mean(pooled, axis=1, keepdims=True)
    return away, lax.rsqrt(jnp.mean(away * away, axis=1, keepdims=True) + EPS)


def head_body(here_ref, p0, p1, p2, p3, target_ref, weight_ref, w_ref, pooled_ref, part_ref, send_ref):
    here = here_ref[0]
    parts = [p[...] for p in (p0, p1, p2, p3)]
    for j in range(4):
        pooled_ref[j : j + 1, :] = in_order(here, parts, j) * (1.0 / PATCHES)
    away, scale = centered(pooled_ref[...])
    normed = (away * scale).astype(BF16)
    logits = dot(normed, w_ref[...], 1, 0)
    hit = target_ref[...] > 0.5
    signed = jnp.where(hit, -logits, logits)
    small = jnp.exp(-jnp.abs(signed))
    nll = jnp.maximum(signed, 0.0) + jnp.log1p(small)
    inverse = 1.0 / (1.0 + small)
    miss = jnp.where(signed >= 0.0, 1.0, small) * inverse
    keep = jnp.where(signed >= 0.0, small, 1.0) * inverse
    weight = weight_ref[...]
    loss = jnp.sum(weight * (miss * miss) * nll, axis=1, keepdims=True)
    slope = weight * (2.0 * miss * keep * nll + miss * miss) * miss
    d_logits = jnp.where(hit, -slope, slope).astype(BF16)
    part_ref[:, :D] = dot(d_logits, w_ref[...], 1, 1)
    part_ref[:, D:] = jnp.broadcast_to(loss, (4, 128))
    zeros = jnp.zeros((4, 48), BF16)
    for d in range(16):
        send_ref[d, :, :COLS] = d_logits
        send_ref[d, :, COLS : COLS + 128] = jnp.concatenate(
            [normed[:, 80 * d : 80 * d + 80], zeros], axis=1
        )


def pooled_body(here_ref, m0, m1, m2, m3, pooled_ref, d_ref, loss_ref):
    here = here_ref[0]
    parts = [m[...] for m in (m0, m1, m2, m3)]
    total = in_order(here, parts, 0)
    for j in (1, 2, 3):
        total = total + in_order(here, parts, j)
    away, scale = centered(pooled_ref[...])
    normed = away * scale
    d_normed = total[:, :D]
    mean = jnp.mean(d_normed, axis=1, keepdims=True)
    along = jnp.mean(d_normed * normed, axis=1, keepdims=True)
    d_ref[...] = scale * (d_normed - mean - normed * along)
    loss_ref[...] = total[:, D:]


def effective_of(counts):
    return (1.0 - BETA) / (1.0 - jnp.power(BETA, counts + 1.0))


def label_terms(labels, flat):
    entry = jnp.arange(IMAGES * 4, dtype=I32)
    same = flat[:, None] == flat[None, :]
    sooner = entry[:, None] > entry[None, :]
    same_image = (entry[:, None] // 4) == (entry[None, :] // 4)
    fresh = ~jnp.any(same & sooner & same_image, axis=1)
    first = ~jnp.any(same & sooner, axis=1)
    entry_count = jnp.sum((same & fresh[None, :]).astype(F32), axis=1)
    distinct = jnp.sum(first.astype(F32))
    effective_total = (CLASSES - distinct) * effective_of(jnp.zeros((), F32)) + jnp.sum(
        jnp.where(first, effective_of(entry_count), 0.0)
    )
    class_ids = lax.axis_index(EX) * COLS + jnp.arange(COLS, dtype=I32)
    targets = jnp.any(labels[:, :, None] == class_ids[None, None, :], axis=1).astype(F32)
    counts = jnp.sum(((flat[:, None] == class_ids[None, :]) & fresh[:, None]).astype(F32), axis=0)
    return targets, (effective_of(counts) * CLASSES / effective_total).reshape(1, COLS)


def chip_swap(packed, after=None):
    packed = packed.reshape(CHIPS, CAP // 2, 2, D)
    if after is not None:
        packed, _ = lax.optimization_barrier((packed, after))
    return lax.all_to_all(packed, CHIP, 0, 0, tiled=True).reshape(PACKED)


def shards(tokens, routes, combine, w_in, w_out, out_grad, head_w, labels):
    here = lax.axis_index(Y).astype(I32).reshape(1)
    table, x_send = run(
        x_body,
        (shape((2, TOK, HALF), BF16), shape(PACKED, BF16)),
        routes,
        tokens,
        name="dispatch_x",
    )
    x_in = chip_swap(x_send)
    g_send = run(g_body, shape(PACKED, BF16), table, out_grad, combine, name="dispatch_g")
    all_labels = dp_gather(labels).reshape(IMAGES * 4)
    x_in, g_send, all_labels = lax.optimization_barrier((x_in, g_send, all_labels))
    targets, class_weight = label_terms(labels, all_labels)
    g_in = chip_swap(g_send)
    x_other = lax.ppermute(x_in, "core", SWAP)
    halves = (shape((HALF, D), F32), shape((HALF, D), BF16))
    whole = (shape(SQUARE, BF16), shape(SQUARE, BF16))
    xs, hidden, slope, own, other = run(
        forward_body,
        (*whole, shape(SQUARE, BF16), *halves),
        x_in,
        x_other,
        w_in,
        w_out,
        specs=[VMEM, VMEM, ANY, ANY],
        scratch=WEIGHTS,
        name="forward",
    )
    g_in, own, other, targets, class_weight = lax.optimization_barrier(
        (g_in, own, other, targets, class_weight)
    )
    out_send = add_cores(own, other, "add_out")
    out_in = chip_swap(out_send)
    g_other = lax.ppermute(g_in, "core", SWAP)
    gs, d_pre, own, other = run(
        backward_body,
        (*whole, *halves),
        g_in,
        g_other,
        slope,
        w_in,
        w_out,
        specs=[VMEM, VMEM, VMEM, ANY, ANY],
        scratch=WEIGHTS,
        name="backward",
    )
    out_in, own, other = lax.optimization_barrier((out_in, own, other))
    rows_send = add_cores(own, other, "add_rows")
    rows_in = chip_swap(rows_send)
    mixed_out, d_combine, token_sum = run(
        mixed_body,
        (shape((TOK, D), BF16), shape((TOK, 2), F32), shape((1, D), F32)),
        table,
        out_in,
        tokens,
        out_grad,
        combine,
        name="mixed",
    )
    sums = y_parts(lax.psum(token_sum, "core"))
    pooled, part, dp_send = run(
        head_body,
        (shape((4, D), F32), shape((4, D + 128), F32), shape((16, 4, COLS + 128), BF16)),
        here,
        *sums,
        targets,
        class_weight,
        head_w,
        specs=[SMEM] + [VMEM] * 7,
        name="head",
    )
    messages = y_parts(lax.psum(part, "core"))
    d_pooled, losses = run(
        pooled_body,
        (shape((4, D), F32), shape((4, 128), F32)),
        here,
        *messages,
        pooled,
        specs=[SMEM] + [VMEM] * 5,
        name="d_pooled",
    )
    dp_send, rows_in = lax.optimization_barrier((dp_send, rows_in))
    dp_in = lax.all_to_all(dp_send, "dp", 0, 0, tiled=True).reshape(IMAGES, COLS + 128)
    d_tokens = run(tokens_body, shape((TOK, D), BF16), table, rows_in, out_grad, name="d_tokens")
    d_w_out = dot(hidden, gs, 0, 0).astype(BF16)
    d_w_in = dot(xs, d_pre, 0, 0).astype(BF16)
    d_head = dot(dp_in[:, COLS : COLS + 80], dp_in[:, :COLS], 0, 0).astype(BF16)
    return (mixed_out, d_tokens, d_combine, d_w_in, d_w_out, losses[:, 0], d_pooled, d_head)


def solution(mesh):
    grid = Mesh(mesh.devices.reshape(16, 2, 2, 2), ALL)
    rows = P(ALL, None)
    in_specs = (rows, rows, rows, P(None, ALL), rows, rows, P(None, EX), P("dp", None))
    out_specs = (
        rows,
        rows,
        rows,
        P(None, ALL),
        rows,
        P("dp"),
        P("dp", None),
        P("dp", EX),
    )
    return jax.shard_map(shards, mesh=grid, in_specs=in_specs, out_specs=out_specs, check_vma=False)
```

```python
import math

import jax
import jax.numpy as jnp
from jax import lax
from jax.experimental import pallas as pl
from jax.experimental.pallas import tpu as pltpu
from jax.sharding import Mesh, PartitionSpec as P

D = 1280
EXPERTS = 32
PATCHES = 256
CLASSES = 17408
CAP = 10
CHIPS = 64
IMAGES = 64
TOK = 128
HALF = CHIPS * CAP
ROWS = 2 * HALF
COLS = CLASSES // 8
BETA = 0.99
LOG_BETA = math.log(BETA)
EPS = 1e-06

CHIP = ("dp", "yh", "yl")
Y = ("yh", "yl")
EX = ("yh", "yl", "core")
ALL = ("dp", "yh", "yl", "core")
SWAP = [(0, 1), (1, 0)]
F32 = jnp.float32
BF16 = jnp.bfloat16
I32 = jnp.int32
PACKED = (HALF // 2, 2, D)
WIDE = D + 128
PACKED_X = (HALF // 2, 2, WIDE)
ROOT_2_PI = 0.7978845608028654
CUBIC = 0.044715


def dot(a, b, ca, cb):
    return lax.dot_general(a, b, (((ca,), (cb,)), ((), ())), preferred_element_type=F32)


def shape(dims, dtype):
    return jax.ShapeDtypeStruct(dims, dtype)


VMEM = pl.BlockSpec(memory_space=pltpu.VMEM)
SMEM = pl.BlockSpec(memory_space=pltpu.SMEM)
ANY = pl.BlockSpec(memory_space=pl.ANY)


TINY = pl.CostEstimate(flops=1, transcendentals=0, bytes_accessed=1)


LONG = pl.CostEstimate(flops=1 << 34, transcendentals=0, bytes_accessed=1 << 26)


def run(body, outs, *args, specs=None, out_specs=None, scratch=(), name=None, cost=TINY):
    return pl.pallas_call(
        body,
        out_shape=outs,
        in_specs=specs or [VMEM] * len(args),
        out_specs=out_specs or jax.tree.map(lambda _: VMEM, outs),
        scratch_shapes=list(scratch),
        name=name,
        cost_estimate=cost,
        compiler_params=pltpu.CompilerParams(vmem_limit_bytes=56 << 20),
    )(*args)


def pack_rows(ref, value):
    ref[...] = value.astype(BF16).reshape(ref.shape)


def x_body(routes_ref, labels_ref, tokens_ref, table_ref, send_ref):
    ids = lax.broadcasted_iota(I32, (EXPERTS, TOK), 0)
    routes = (routes_ref[0:1, :], routes_ref[1:2, :])
    hit = [r == ids for r in routes]
    hits = jnp.where(hit[0], 1.0, jnp.where(hit[1], 1.0, 0.0)).astype(BF16)
    t_row = lax.broadcasted_iota(I32, (TOK, TOK), 0)
    t_col = lax.broadcasted_iota(I32, (TOK, TOK), 1)
    before = jnp.where(t_row < t_col, 1.0, 0.0).astype(BF16)
    earlier = dot(hits, before, 1, 0)
    slot = lax.broadcasted_iota(I32, (HALF, TOK), 0)
    both = jnp.zeros((HALF, TOK), F32)
    for k in range(2):
        pos = jnp.sum(jnp.where(hit[k], earlier, 0.0), axis=0, keepdims=True)
        row = routes[k] * (2 * CAP) + pos.astype(I32)
        table = jnp.where(slot == row, 1.0, jnp.where(slot == row + CAP, 1.0, 0.0))
        table_ref[k] = table.astype(BF16)
        both = both + table
    rows = dot(both.astype(BF16), tokens_ref[...], 1, 0)
    labels = labels_ref[...]
    high = lax.shift_right_logical(labels, 8)
    low = labels - high * 256
    digits = jnp.concatenate(
        [high.astype(F32), low.astype(F32), jnp.zeros((4, 120), F32)], axis=1
    ).astype(BF16)
    place = lax.broadcasted_iota(I32, (HALF, 4), 0)
    image = lax.broadcasted_iota(I32, (HALF, 4), 1)
    chip = lax.shift_right_logical(place * 6554, 16)
    spread = jnp.where(place - CAP * chip == image, 1.0, 0.0).astype(BF16)
    pack_rows(send_ref, jnp.concatenate([rows, dot(spread, digits, 1, 0)], axis=1))


def g_body(table_ref, grad_ref, combine_ref, send_ref):
    table0, table1 = table_ref[0].astype(F32), table_ref[1].astype(F32)
    scale = jnp.sum(
        table0 * combine_ref[0:1, :] + table1 * combine_ref[1:2, :], axis=1, keepdims=True
    )
    pack_rows(send_ref, scale * dot((table0 + table1).astype(BF16), grad_ref[...], 1, 0))


CHUNK = 320
STEPS = HALF // CHUNK


def chunk_rows(base, i):
    return pl.ds(pl.multiple_of(base + i * CHUNK, CHUNK), CHUNK)


def chunk_copies(i, square, own, other, sems):
    pairs = []
    for vmem, hbm in square:
        for base in (0, HALF):
            rows = chunk_rows(base, i)
            pairs.append((vmem.at[rows, :], hbm.at[rows, :]))
    for vmem, hbm in (own, other):
        rows = chunk_rows(0, i)
        pairs.append((vmem.at[rows, :], hbm.at[rows, :]))
    return [pltpu.make_async_copy(s, d, sems.at[i, n]) for n, (s, d) in enumerate(pairs)]


def load(pairs, sems):
    copies = [pltpu.make_async_copy(s, d, sems.at[n]) for n, (s, d) in enumerate(pairs)]
    for copy in copies:
        copy.start()
    return copies


def forward_body(
    own_in, other_in, w1_in, w2_in, xs_out, hidden_out, slope_out, own_out, other_out,
    own_x, other_x, w1, w2, xs, hidden, slope, own, other, in_sems, xs_sem, out_sems,
):
    copies = load(((own_in, own_x), (other_in, other_x), (w1_in, w1), (w2_in, w2)), in_sems)
    copies[0].wait()
    xs[:HALF] = own_x[:, :, :D].reshape(HALF, D)
    copies[1].wait()
    xs[HALF:] = other_x[:, :, :D].reshape(HALF, D)
    keep = pltpu.make_async_copy(xs, xs_out, xs_sem)
    keep.start()
    copies[2].wait()
    copies[3].wait()

    def outputs(i):
        square = ((hidden, hidden_out), (slope, slope_out))
        return chunk_copies(i, square, (own, own_out), (other, other_out), out_sems)

    def step(i, carry):
        for base in (0, HALF):
            rows = chunk_rows(base, i)
            h = dot(xs[rows, :], w1[...], 1, 0)
            square = h * h
            bend = jnp.tanh(ROOT_2_PI * h * (1.0 + CUBIC * square))
            half = 0.5 * (1.0 + bend)
            act = (h * half).astype(BF16)
            hidden[rows, :] = act
            slope[rows, :] = (
                half
                + 0.5 * h * (1.0 - bend * bend) * (ROOT_2_PI * (1.0 + 3.0 * CUBIC * square))
            ).astype(BF16)
            part = dot(act, w2[...], 1, 0)
            if base == 0:
                own[chunk_rows(0, i), :] = part
            else:
                other[chunk_rows(0, i), :] = part.astype(BF16)
        for copy in outputs(i):
            copy.start()
        return carry

    lax.fori_loop(0, STEPS, step, 0)
    keep.wait()
    for i in range(STEPS):
        for copy in outputs(i):
            copy.wait()


def backward_body(
    own_in, other_in, slope_in, w1_in, w2_in, gs_out, d_pre_out, own_out, other_out,
    own_g, other_g, slope, w1, w2, gs, d_pre, own, other, in_sems, gs_sem, out_sems,
):
    pairs = ((own_in, own_g), (other_in, other_g), (w2_in, w2), (slope_in, slope), (w1_in, w1))
    copies = load(pairs, in_sems)
    copies[0].wait()
    gs[:HALF] = own_g[...].reshape(HALF, D)
    copies[1].wait()
    gs[HALF:] = other_g[...].reshape(HALF, D)
    keep = pltpu.make_async_copy(gs, gs_out, gs_sem)
    keep.start()
    for copy in copies[2:]:
        copy.wait()

    def outputs(i):
        square = ((d_pre, d_pre_out),)
        return chunk_copies(i, square, (own, own_out), (other, other_out), out_sems)

    def step(i, carry):
        for base in (0, HALF):
            rows = chunk_rows(base, i)
            d_h = dot(gs[rows, :], w2[...], 1, 1)
            act = (d_h * slope[rows, :].astype(F32)).astype(BF16)
            d_pre[rows, :] = act
            part = dot(act, w1[...], 1, 1)
            if base == 0:
                own[chunk_rows(0, i), :] = part
            else:
                other[chunk_rows(0, i), :] = part.astype(BF16)
        for copy in outputs(i):
            copy.start()
        return carry

    lax.fori_loop(0, STEPS, step, 0)
    keep.wait()
    for i in range(STEPS):
        for copy in outputs(i):
            copy.wait()


SQUARE = (ROWS, D)


def expert_kernel(body, ins, kept, received, name):
    outs = (*[shape(SQUARE, BF16)] * kept, shape((HALF, D), F32), shape((HALF, D), BF16))
    scratch = [pltpu.VMEM(received, BF16)] * 2
    scratch += [pltpu.VMEM((D, D), BF16)] * (len(ins) - 2)
    scratch += [pltpu.VMEM(SQUARE, BF16)] * (kept if len(ins) == 4 else 2)
    scratch += [pltpu.VMEM((HALF, D), F32), pltpu.VMEM((HALF, D), BF16)]
    scratch += [
        pltpu.SemaphoreType.DMA((len(ins),)),
        pltpu.SemaphoreType.DMA,
        pltpu.SemaphoreType.DMA((STEPS, 6)),
    ]
    return run(
        body,
        outs,
        *ins,
        specs=[ANY] * len(ins),
        out_specs=tuple([ANY] * len(outs)),
        scratch=scratch,
        name=name,
    )


GRAD_COLS = 256


def weight_grad_body(left_ref, right_ref, out_ref):
    def step(i, carry):
        cols = pl.ds(pl.multiple_of(i * GRAD_COLS, GRAD_COLS), GRAD_COLS)
        out_ref[cols, :] = dot(left_ref[:, cols], right_ref[...], 0, 0).astype(BF16)
        return carry

    lax.fori_loop(0, D // GRAD_COLS, step, 0)


def add_body(own_ref, other_ref, send_ref):
    pack_rows(send_ref, own_ref[...] + other_ref[...].astype(F32))


def across(row):
    return jnp.sum(jnp.where(eye(), row, 0.0), axis=1, keepdims=True)


def along(column):
    return jnp.sum(jnp.where(eye(), column, 0.0), axis=0, keepdims=True)


def eye():
    return lax.broadcasted_iota(I32, (TOK, TOK), 0) == lax.broadcasted_iota(I32, (TOK, TOK), 1)


def mixed_body(table_ref, in_ref, tokens_ref, grad_ref, combine_ref, mixed_ref, dc_ref, sum_ref):
    rows = in_ref[...].reshape(HALF, D)
    vals0 = dot(table_ref[0], rows, 0, 0)
    vals1 = dot(table_ref[1], rows, 0, 0)
    grad = grad_ref[...].astype(F32)
    dc_ref[0:1, :] = along(jnp.sum(grad * vals0, axis=1, keepdims=True))
    dc_ref[1:2, :] = along(jnp.sum(grad * vals1, axis=1, keepdims=True))
    mixed = (
        tokens_ref[...].astype(F32)
        + (across(combine_ref[0:1, :]) * vals0 + across(combine_ref[1:2, :]) * vals1)
    ).astype(BF16)
    mixed_ref[...] = mixed
    sum_ref[...] = jnp.sum(mixed.astype(F32), axis=0, keepdims=True)


def tokens_body(table_ref, in_ref, grad_ref, out_ref):
    rows = in_ref[...].reshape(HALF, D)
    table = (table_ref[0].astype(F32) + table_ref[1].astype(F32)).astype(BF16)
    out_ref[...] = (grad_ref[...].astype(F32) + dot(table, rows, 0, 0)).astype(BF16)


def in_order(here, parts, j):
    pick = parts[0]
    for shift in (1, 2, 3):
        pick = jnp.where((here + shift) % 4 == j, parts[shift], pick)
    return pick


def y_parts(mine):
    return [mine] + [
        lax.ppermute(mine, Y, [((i + shift) % 4, i) for i in range(4)]) for shift in (1, 2, 3)
    ]


def centered(pooled):
    away = pooled - jnp.mean(pooled, axis=1, keepdims=True)
    return away, lax.rsqrt(jnp.mean(away * away, axis=1, keepdims=True) + EPS)


def head_body(here_ref, p0, p1, p2, p3, target_ref, weight_ref, w_ref, pooled_ref, part_ref, send_ref):
    here = here_ref[0]
    parts = [p[...] for p in (p0, p1, p2, p3)]
    for j in range(4):
        pooled_ref[j : j + 1, :] = in_order(here, parts, j) * (1.0 / PATCHES)
    away, scale = centered(pooled_ref[...])
    normed = (away * scale).astype(BF16)
    logits = dot(normed, w_ref[...], 1, 0)
    hit = target_ref[...] > 0.5
    signed = jnp.where(hit, -logits, logits)
    small = jnp.exp(-jnp.abs(signed))
    nll = jnp.maximum(signed, 0.0) + jnp.log1p(small)
    inverse = 1.0 / (1.0 + small)
    miss = jnp.where(signed >= 0.0, 1.0, small) * inverse
    keep = jnp.where(signed >= 0.0, small, 1.0) * inverse
    weight = weight_ref[...]
    loss = jnp.sum(weight * (miss * miss) * nll, axis=1, keepdims=True)
    slope = weight * (2.0 * miss * keep * nll + miss * miss) * miss
    d_logits = jnp.where(hit, -slope, slope).astype(BF16)
    part_ref[:, :D] = dot(d_logits, w_ref[...], 1, 1)
    part_ref[:, D:] = jnp.broadcast_to(loss, (4, 128))
    zeros = jnp.zeros((4, 48), BF16)
    for d in range(16):
        send_ref[d, :, :COLS] = d_logits
        send_ref[d, :, COLS : COLS + 128] = jnp.concatenate(
            [normed[:, 80 * d : 80 * d + 80], zeros], axis=1
        )


def pooled_body(here_ref, m0, m1, m2, m3, pooled_ref, d_ref, loss_ref):
    here = here_ref[0]
    parts = [m[...] for m in (m0, m1, m2, m3)]
    total = in_order(here, parts, 0)
    for j in (1, 2, 3):
        total = total + in_order(here, parts, j)
    away, scale = centered(pooled_ref[...])
    normed = away * scale
    d_normed = total[:, :D]
    mean = jnp.mean(d_normed, axis=1, keepdims=True)
    along = jnp.mean(d_normed * normed, axis=1, keepdims=True)
    d_ref[...] = scale * (d_normed - mean - normed * along)
    loss_ref[...] = total[:, D:]


def effective_of(counts):
    return (1.0 - BETA) / (1.0 - jnp.exp((counts + 1.0) * LOG_BETA))


def label_body(first_ref, digits_ref, labels_ref, target_ref, weight_ref):
    ids = (lax.broadcasted_iota(I32, (1, COLS), 1) + first_ref[0]).astype(F32)
    own = labels_ref[...].astype(F32)
    target = own[:, 0:1] == ids
    for n in range(1, 4):
        target = target | (own[:, n : n + 1] == ids)
    target_ref[...] = jnp.where(target, 1.0, 0.0)
    digits = digits_ref[...].astype(F32)
    labels = digits[:, 0:4] * 256.0 + digits[:, 4:8]
    padded = jnp.concatenate([labels, jnp.zeros((IMAGES, 124), F32)], axis=1)
    turned = jnp.concatenate([padded, jnp.zeros((128 - IMAGES, 128), F32)], axis=0).T
    columns = [labels[:, n : n + 1] for n in range(4)]
    rows = [turned[n : n + 1, :IMAGES] for n in range(4)]

    def fresh_of(entries):
        out = [jnp.ones_like(entries[0])]
        for n in range(1, 4):
            keep = out[0]
            for m in range(n):
                keep = jnp.where(entries[m] == entries[n], 0.0, keep)
            out.append(keep)
        return out

    fresh, fresh_row = fresh_of(columns), fresh_of(rows)
    counts = jnp.zeros((IMAGES, COLS), F32)
    excess = jnp.zeros((IMAGES, 1), F32)
    base = effective_of(jnp.zeros((IMAGES, 1), F32))
    for n in range(4):
        counts = counts + jnp.where(columns[n] == ids, fresh[n], 0.0)
        same = jnp.zeros((IMAGES, IMAGES), F32)
        for m in range(4):
            same = same + jnp.where(columns[n] == rows[m], fresh_row[m], 0.0)
        count = jnp.sum(same, axis=1, keepdims=True)
        excess = excess + fresh[n] * (effective_of(count) - base) / count
    total = CLASSES * base[0:1, :] + jnp.sum(excess, axis=0, keepdims=True)
    weight_ref[...] = effective_of(jnp.sum(counts, axis=0, keepdims=True)) * (CLASSES / total)


def chip_swap(packed):
    dims = packed.shape
    blocks = packed.reshape(CHIPS, CAP // 2, 2, dims[-1])
    return lax.all_to_all(blocks, CHIP, 0, 0, tiled=True).reshape(dims)


def core_swap(rows):
    return lax.ppermute(rows, "core", SWAP)


def shards(tokens, routes, combine, w_in, w_out, out_grad, head_w, labels):
    here = lax.axis_index(Y).astype(I32).reshape(1)
    first_class = (lax.axis_index(EX) * COLS).astype(I32).reshape(1)
    combine = combine.T
    table, x_send = run(
        x_body,
        (shape((2, HALF, TOK), BF16), shape(PACKED_X, BF16)),
        routes.T,
        labels,
        tokens,
        name="dispatch_x",
    )
    x_in = chip_swap(x_send)
    g_send = run(g_body, shape(PACKED, BF16), table, out_grad, combine, name="dispatch_g")
    x_in, g_send = lax.optimization_barrier((x_in, g_send))
    g_in = chip_swap(g_send)
    xs, hidden, slope, own, other = expert_kernel(
        forward_body, (x_in, core_swap(x_in), w_in, w_out), 3, PACKED_X, "forward"
    )
    other = core_swap(other)
    digits = x_in.reshape(IMAGES // 4, 4, CAP, WIDE)[:, 0, :4, D : D + 128].reshape(IMAGES, 128)
    g_in, digits = lax.optimization_barrier((g_in, digits))
    targets, class_weight = run(
        label_body,
        (shape((4, COLS), F32), shape((1, COLS), F32)),
        first_class,
        digits,
        labels,
        specs=[SMEM, VMEM, VMEM],
        name="labels",
        cost=LONG,
    )
    own, class_weight = lax.optimization_barrier((own, class_weight))
    out_in = chip_swap(run(add_body, shape(PACKED, BF16), own, other, name="add_out"))
    gs, d_pre, own, other = expert_kernel(
        backward_body, (g_in, core_swap(g_in), slope, w_in, w_out), 2, PACKED, "backward"
    )
    other = core_swap(other)
    d_w_out = run(weight_grad_body, shape((D, D), BF16), hidden, gs, name="d_w_out")
    out_in, d_w_out = lax.optimization_barrier((out_in, d_w_out))
    mixed_out, d_combine, token_sum = run(
        mixed_body,
        (shape((TOK, D), BF16), shape((2, TOK), F32), shape((1, D), F32)),
        table,
        out_in,
        tokens,
        out_grad,
        combine,
        name="mixed",
        cost=LONG,
    )
    own, token_sum = lax.optimization_barrier((own, token_sum))
    rows_in = chip_swap(run(add_body, shape(PACKED, BF16), own, other, name="add_rows"))
    sums = y_parts(lax.psum(token_sum, "core"))
    pooled, part, dp_send = run(
        head_body,
        (shape((4, D), F32), shape((4, D + 128), F32), shape((16, 4, COLS + 128), BF16)),
        here,
        *sums,
        targets,
        class_weight,
        head_w,
        specs=[SMEM] + [VMEM] * 7,
        name="head",
    )
    messages = y_parts(lax.psum(part, "core"))
    d_pooled, losses = run(
        pooled_body,
        (shape((4, D), F32), shape((4, 128), F32)),
        here,
        *messages,
        pooled,
        specs=[SMEM] + [VMEM] * 5,
        name="d_pooled",
    )
    dp_send, rows_in, xs, d_pooled = lax.optimization_barrier((dp_send, rows_in, xs, d_pooled))
    dp_in = lax.all_to_all(dp_send, "dp", 0, 0, tiled=True).reshape(IMAGES, COLS + 128)
    d_tokens = run(tokens_body, shape((TOK, D), BF16), table, rows_in, out_grad, name="d_tokens")
    d_w_in = run(weight_grad_body, shape((D, D), BF16), xs, d_pre, name="d_w_in")
    d_head = dot(dp_in[:, COLS : COLS + 80], dp_in[:, :COLS], 0, 0).astype(BF16)
    return (mixed_out, d_tokens, d_combine.T, d_w_in, d_w_out, losses[:, 0], d_pooled, d_head)


def solution(mesh):
    grid = Mesh(mesh.devices.reshape(16, 2, 2, 2), ALL)
    rows = P(ALL, None)
    in_specs = (rows, rows, rows, P(None, ALL), rows, rows, P(None, EX), P("dp", None))
    out_specs = (
        rows,
        rows,
        rows,
        P(None, ALL),
        rows,
        P("dp"),
        P("dp", None),
        P("dp", EX),
    )
    return jax.shard_map(shards, mesh=grid, in_specs=in_specs, out_specs=out_specs, check_vma=False)
```

```python
import math

import jax
import jax.numpy as jnp
from jax import lax
from jax.experimental import pallas as pl
from jax.experimental.pallas import tpu as pltpu
from jax.sharding import Mesh, PartitionSpec as P

D = 1280
EXPERTS = 32
PATCHES = 256
CLASSES = 17408
CAP = 10
CHIPS = 64
IMAGES = 64
TOK = 128
HALF = CHIPS * CAP
ROWS = 2 * HALF
COLS = CLASSES // 8
BETA = 0.99
LOG_BETA = math.log(BETA)
EPS = 1e-06

CHIP = ("dp", "yh", "yl")
Y = ("yh", "yl")
EX = ("yh", "yl", "core")
ALL = ("dp", "yh", "yl", "core")
SWAP = [(0, 1), (1, 0)]
F32 = jnp.float32
BF16 = jnp.bfloat16
I32 = jnp.int32
PACKED = (HALF // 2, 2, D)
WIDE = D + 128
PACKED_X = (HALF // 2, 2, WIDE)
ROOT_2_PI = 0.7978845608028654
CUBIC = 0.044715


def dot(a, b, ca, cb):
    return lax.dot_general(a, b, (((ca,), (cb,)), ((), ())), preferred_element_type=F32)


def shape(dims, dtype):
    return jax.ShapeDtypeStruct(dims, dtype)


VMEM = pl.BlockSpec(memory_space=pltpu.VMEM)
SMEM = pl.BlockSpec(memory_space=pltpu.SMEM)
ANY = pl.BlockSpec(memory_space=pl.ANY)


TINY = pl.CostEstimate(flops=1, transcendentals=0, bytes_accessed=1)


LONG = pl.CostEstimate(flops=1 << 34, transcendentals=0, bytes_accessed=1 << 26)


def run(body, outs, *args, grid=(), specs=None, out_specs=None, scratch=(), name=None, cost=TINY):
    return pl.pallas_call(
        body,
        out_shape=outs,
        grid=grid,
        in_specs=specs or [VMEM] * len(args),
        out_specs=out_specs or jax.tree.map(lambda _: VMEM, outs),
        scratch_shapes=list(scratch),
        name=name,
        cost_estimate=cost,
        compiler_params=pltpu.CompilerParams(vmem_limit_bytes=56 << 20),
    )(*args)


def pack_rows(ref, value):
    ref[...] = value.astype(BF16).reshape(ref.shape)


def x_body(routes_ref, labels_ref, tokens_ref, table_ref, send_ref):
    ids = lax.broadcasted_iota(I32, (EXPERTS, TOK), 0)
    routes = (routes_ref[0:1, :], routes_ref[1:2, :])
    hit = [r == ids for r in routes]
    hits = jnp.where(hit[0], 1.0, jnp.where(hit[1], 1.0, 0.0)).astype(BF16)
    t_row = lax.broadcasted_iota(I32, (TOK, TOK), 0)
    t_col = lax.broadcasted_iota(I32, (TOK, TOK), 1)
    before = jnp.where(t_row < t_col, 1.0, 0.0).astype(BF16)
    earlier = dot(hits, before, 1, 0)
    slot = lax.broadcasted_iota(I32, (HALF, TOK), 0)
    both = jnp.zeros((HALF, TOK), F32)
    for k in range(2):
        pos = jnp.sum(jnp.where(hit[k], earlier, 0.0), axis=0, keepdims=True)
        row = routes[k] * (2 * CAP) + pos.astype(I32)
        table = jnp.where(slot == row, 1.0, jnp.where(slot == row + CAP, 1.0, 0.0))
        table_ref[k] = table.astype(BF16)
        both = both + table
    rows = dot(both.astype(BF16), tokens_ref[...], 1, 0)
    labels = labels_ref[...]
    high = lax.shift_right_logical(labels, 8)
    low = labels - high * 256
    digits = jnp.concatenate(
        [high.astype(F32), low.astype(F32), jnp.zeros((4, 120), F32)], axis=1
    ).astype(BF16)
    place = lax.broadcasted_iota(I32, (HALF, 4), 0)
    image = lax.broadcasted_iota(I32, (HALF, 4), 1)
    chip = lax.shift_right_logical(place * 6554, 16)
    spread = jnp.where(place - CAP * chip == image, 1.0, 0.0).astype(BF16)
    pack_rows(send_ref, jnp.concatenate([rows, dot(spread, digits, 1, 0)], axis=1))


def g_body(table_ref, grad_ref, combine_ref, send_ref):
    table0, table1 = table_ref[0].astype(F32), table_ref[1].astype(F32)
    scale = jnp.sum(
        table0 * combine_ref[0:1, :] + table1 * combine_ref[1:2, :], axis=1, keepdims=True
    )
    pack_rows(send_ref, scale * dot((table0 + table1).astype(BF16), grad_ref[...], 1, 0))


HALVES = (slice(0, HALF), slice(HALF, ROWS))


def chunks(part, size):
    return [slice(n, n + size) for n in range(part.start, part.stop, size)]


def start_all(pairs, sems):
    copies = [pltpu.make_async_copy(s, d, sems.at[n]) for n, (s, d) in enumerate(pairs)]
    for copy in copies:
        copy.start()
    return copies


def forward_body(
    own_in, other_in, w1_in, w2_in, xs_out, hidden_out, slope_out, own_out, other_out,
    own_x, other_x, w1, w2, xs, hidden, slope, own, other, in_sems, out_sems,
):
    pairs = ((own_in, own_x), (w1_in, w1), (other_in, other_x), (w2_in, w2))
    copies = start_all(pairs, in_sems)
    saved = []
    for n, half in enumerate(HALVES):
        copies[2 * n].wait()
        xs[half] = (own_x, other_x)[n][:, :, :D].reshape(HALF, D)
        if n == 0:
            copies[1].wait()
        for rows in chunks(half, 160):
            h = dot(xs[rows, :], w1[...], 1, 0)
            square = h * h
            bend = jnp.tanh(h * (ROOT_2_PI + (ROOT_2_PI * CUBIC) * square))
            act = 0.5 + 0.5 * bend
            hidden[rows, :] = (h * act).astype(BF16)
            tilt = (1.0 - bend * bend) * (0.5 * ROOT_2_PI + (1.5 * ROOT_2_PI * CUBIC) * square)
            slope[rows, :] = (act + h * tilt).astype(BF16)
        saved += start_all(
            [(v.at[half], o.at[half]) for v, o in ((xs, xs_out), (hidden, hidden_out), (slope, slope_out))],
            out_sems.at[n],
        )
        if n == 0:
            copies[3].wait()
        for rows in chunks(half, 160):
            part = dot(hidden[rows, :], w2[...], 1, 0)
            there = slice(rows.start - half.start, rows.stop - half.start)
            if n == 0:
                own[there, :] = part
            else:
                other[there, :] = part.astype(BF16)
        saved += start_all([((own, other)[n], (own_out, other_out)[n])], out_sems.at[2 + n])
    for copy in saved:
        copy.wait()


def backward_body(
    own_in, other_in, slope_in, w1_in, w2_in, gs_out, d_pre_out, own_out, other_out,
    own_g, other_g, slope, w1, w2, gs, d_pre, own, other, in_sems, out_sems,
):
    first, last = HALVES
    pairs = (
        (own_in, own_g), (w2_in, w2), (slope_in.at[first], slope.at[first]), (w1_in, w1),
        (other_in, other_g), (slope_in.at[last], slope.at[last]),
    )
    copies = start_all(pairs, in_sems)
    saved = []
    for n, half in enumerate(HALVES):
        copies[4 * n].wait()
        gs[half] = (own_g, other_g)[n][...].reshape(HALF, D)
        if n == 0:
            copies[1].wait()
        copies[(2, 5)[n]].wait()
        for rows in chunks(half, 320):
            d_h = dot(gs[rows, :], w2[...], 1, 1)
            d_pre[rows, :] = (d_h * slope[rows, :].astype(F32)).astype(BF16)
        saved += start_all(
            [(v.at[half], o.at[half]) for v, o in ((gs, gs_out), (d_pre, d_pre_out))],
            out_sems.at[n],
        )
        if n == 0:
            copies[3].wait()
        for rows in chunks(half, 320):
            part = dot(d_pre[rows, :], w1[...], 1, 1)
            there = slice(rows.start - half.start, rows.stop - half.start)
            if n == 0:
                own[there, :] = part
            else:
                other[there, :] = part.astype(BF16)
        saved += start_all([((own, other)[n], (own_out, other_out)[n])], out_sems.at[2 + n])
    for copy in saved:
        copy.wait()


SQUARE = (ROWS, D)


def expert_kernel(body, ins, kept, received, name):
    outs = (*[shape(SQUARE, BF16)] * kept, shape((HALF, D), F32), shape((HALF, D), BF16))
    scratch = [pltpu.VMEM(received, BF16)] * 2
    scratch += [pltpu.VMEM((D, D), BF16)] * (len(ins) - 2)
    scratch += [pltpu.VMEM(SQUARE, BF16)] * (kept if len(ins) == 4 else 2)
    scratch += [pltpu.VMEM((HALF, D), F32), pltpu.VMEM((HALF, D), BF16)]
    scratch += [
        pltpu.SemaphoreType.DMA((6,)),
        pltpu.SemaphoreType.DMA((4, 3)),
    ]
    return run(
        body,
        outs,
        *ins,
        specs=[ANY] * len(ins),
        out_specs=tuple([ANY] * len(outs)),
        scratch=scratch,
        name=name,
    )


GRAD_COLS = 640


def weight_grad_body(left_ref, right_ref, out_ref):
    out_ref[...] = dot(left_ref[...], right_ref[...], 0, 0).astype(BF16)


def weight_grad(left, right, name):
    return run(
        weight_grad_body,
        shape((D, D), BF16),
        left,
        right,
        grid=(D // GRAD_COLS,),
        specs=[pl.BlockSpec((ROWS, GRAD_COLS), lambda i: (0, i)), pl.BlockSpec((ROWS, D), lambda i: (0, 0))],
        out_specs=pl.BlockSpec((GRAD_COLS, D), lambda i: (i, 0)),
        name=name,
    )


def add_body(own_ref, other_ref, send_ref):
    pack_rows(send_ref, own_ref[...] + other_ref[...].astype(F32))


ADD_ROWS = 320


def add_cores(own, other, name):
    rows = pl.BlockSpec((ADD_ROWS, D), lambda i: (i, 0))
    return run(
        add_body,
        shape(PACKED, BF16),
        own,
        other,
        grid=(HALF // ADD_ROWS,),
        specs=[rows, rows],
        out_specs=pl.BlockSpec((ADD_ROWS // 2, 2, D), lambda i: (i, 0, 0)),
        name=name,
    )


def across(row):
    return jnp.sum(jnp.where(eye(), row, 0.0), axis=1, keepdims=True)


def along(column):
    return jnp.sum(jnp.where(eye(), column, 0.0), axis=0, keepdims=True)


def eye():
    return lax.broadcasted_iota(I32, (TOK, TOK), 0) == lax.broadcasted_iota(I32, (TOK, TOK), 1)


def mixed_body(table_ref, in_ref, tokens_ref, grad_ref, combine_ref, mixed_ref, dc_ref, sum_ref):
    rows = in_ref[...].reshape(HALF, D)
    vals0 = dot(table_ref[0], rows, 0, 0)
    vals1 = dot(table_ref[1], rows, 0, 0)
    grad = grad_ref[...].astype(F32)
    dc_ref[0:1, :] = along(jnp.sum(grad * vals0, axis=1, keepdims=True))
    dc_ref[1:2, :] = along(jnp.sum(grad * vals1, axis=1, keepdims=True))
    mixed = (
        tokens_ref[...].astype(F32)
        + (across(combine_ref[0:1, :]) * vals0 + across(combine_ref[1:2, :]) * vals1)
    ).astype(BF16)
    mixed_ref[...] = mixed
    sum_ref[...] = jnp.sum(mixed.astype(F32), axis=0, keepdims=True)


def tokens_body(table_ref, in_ref, grad_ref, out_ref):
    rows = in_ref[...].reshape(HALF, D)
    table = (table_ref[0].astype(F32) + table_ref[1].astype(F32)).astype(BF16)
    out_ref[...] = (grad_ref[...].astype(F32) + dot(table, rows, 0, 0)).astype(BF16)


def in_order(here, parts, j):
    pick = parts[0]
    for shift in (1, 2, 3):
        pick = jnp.where((here + shift) % 4 == j, parts[shift], pick)
    return pick


def y_parts(mine):
    return [mine] + [
        lax.ppermute(mine, Y, [((i + shift) % 4, i) for i in range(4)]) for shift in (1, 2, 3)
    ]


def centered(pooled):
    away = pooled - jnp.mean(pooled, axis=1, keepdims=True)
    return away, lax.rsqrt(jnp.mean(away * away, axis=1, keepdims=True) + EPS)


def head_body(here_ref, p0, p1, p2, p3, target_ref, weight_ref, w_ref, pooled_ref, part_ref, send_ref):
    here = here_ref[0]
    parts = [p[...] for p in (p0, p1, p2, p3)]
    for j in range(4):
        pooled_ref[j : j + 1, :] = in_order(here, parts, j) * (1.0 / PATCHES)
    away, scale = centered(pooled_ref[...])
    normed = (away * scale).astype(BF16)
    logits = dot(normed, w_ref[...], 1, 0)
    hit = target_ref[...] > 0.5
    signed = jnp.where(hit, -logits, logits)
    small = jnp.exp(-jnp.abs(signed))
    nll = jnp.maximum(signed, 0.0) + jnp.log1p(small)
    inverse = 1.0 / (1.0 + small)
    miss = jnp.where(signed >= 0.0, 1.0, small) * inverse
    keep = jnp.where(signed >= 0.0, small, 1.0) * inverse
    weight = weight_ref[...]
    loss = jnp.sum(weight * (miss * miss) * nll, axis=1, keepdims=True)
    slope = weight * (2.0 * miss * keep * nll + miss * miss) * miss
    d_logits = jnp.where(hit, -slope, slope).astype(BF16)
    part_ref[:, :D] = dot(d_logits, w_ref[...], 1, 1)
    part_ref[:, D:] = jnp.broadcast_to(loss, (4, 128))
    zeros = jnp.zeros((4, 48), BF16)
    for d in range(16):
        send_ref[d, :, :COLS] = d_logits
        send_ref[d, :, COLS : COLS + 128] = jnp.concatenate(
            [normed[:, 80 * d : 80 * d + 80], zeros], axis=1
        )


def pooled_body(here_ref, m0, m1, m2, m3, pooled_ref, d_ref, loss_ref):
    here = here_ref[0]
    parts = [m[...] for m in (m0, m1, m2, m3)]
    total = in_order(here, parts, 0)
    for j in (1, 2, 3):
        total = total + in_order(here, parts, j)
    away, scale = centered(pooled_ref[...])
    normed = away * scale
    d_normed = total[:, :D]
    mean = jnp.mean(d_normed, axis=1, keepdims=True)
    along = jnp.mean(d_normed * normed, axis=1, keepdims=True)
    d_ref[...] = scale * (d_normed - mean - normed * along)
    diagonal = lax.broadcasted_iota(I32, (4, 4), 0) == lax.broadcasted_iota(I32, (4, 4), 1)
    loss_ref[...] = jnp.sum(
        jnp.where(diagonal, total[:, D : D + 1], 0.0), axis=0, keepdims=True
    )


def effective_of(counts):
    return (1.0 - BETA) / (1.0 - jnp.exp((counts + 1.0) * LOG_BETA))


def label_body(first_ref, digits_ref, labels_ref, target_ref, weight_ref):
    ids = (lax.broadcasted_iota(I32, (1, COLS), 1) + first_ref[0]).astype(F32)
    own = labels_ref[...].astype(F32)
    target = own[:, 0:1] == ids
    for n in range(1, 4):
        target = target | (own[:, n : n + 1] == ids)
    target_ref[...] = jnp.where(target, 1.0, 0.0)
    digits = digits_ref[...].astype(F32)
    labels = digits[:, 0:4] * 256.0 + digits[:, 4:8]
    padded = jnp.concatenate([labels, jnp.zeros((IMAGES, 124), F32)], axis=1)
    turned = jnp.concatenate([padded, jnp.zeros((128 - IMAGES, 128), F32)], axis=0).T
    columns = [labels[:, n : n + 1] for n in range(4)]
    rows = [turned[n : n + 1, :IMAGES] for n in range(4)]

    def fresh_of(entries):
        out = [jnp.ones_like(entries[0])]
        for n in range(1, 4):
            keep = out[0]
            for m in range(n):
                keep = jnp.where(entries[m] == entries[n], 0.0, keep)
            out.append(keep)
        return out

    fresh, fresh_row = fresh_of(columns), fresh_of(rows)
    counts = jnp.zeros((IMAGES, COLS), F32)
    excess = jnp.zeros((IMAGES, 1), F32)
    base = effective_of(jnp.zeros((IMAGES, 1), F32))
    for n in range(4):
        counts = counts + jnp.where(columns[n] == ids, fresh[n], 0.0)
        same = jnp.zeros((IMAGES, IMAGES), F32)
        for m in range(4):
            same = same + jnp.where(columns[n] == rows[m], fresh_row[m], 0.0)
        count = jnp.sum(same, axis=1, keepdims=True)
        excess = excess + fresh[n] * (effective_of(count) - base) / count
    total = CLASSES * base[0:1, :] + jnp.sum(excess, axis=0, keepdims=True)
    weight_ref[...] = effective_of(jnp.sum(counts, axis=0, keepdims=True)) * (CLASSES / total)


def chip_swap(packed):
    dims = packed.shape
    blocks = packed.reshape(CHIPS, CAP // 2, 2, dims[-1])
    return lax.all_to_all(blocks, CHIP, 0, 0, tiled=True).reshape(dims)


def core_swap(rows):
    return lax.ppermute(rows, "core", SWAP)


def shards(tokens, routes, combine, w_in, w_out, out_grad, head_w, labels):
    here = lax.axis_index(Y).astype(I32).reshape(1)
    first_class = (lax.axis_index(EX) * COLS).astype(I32).reshape(1)
    combine = combine.T
    table, x_send = run(
        x_body,
        (shape((2, HALF, TOK), BF16), shape(PACKED_X, BF16)),
        routes.T,
        labels,
        tokens,
        name="dispatch_x",
    )
    x_in = chip_swap(x_send)
    g_send = run(g_body, shape(PACKED, BF16), table, out_grad, combine, name="dispatch_g")
    x_in, g_send = lax.optimization_barrier((x_in, g_send))
    g_in = chip_swap(g_send)
    xs, hidden, slope, own, other = expert_kernel(
        forward_body, (x_in, core_swap(x_in), w_in, w_out), 3, PACKED_X, "forward"
    )
    other = core_swap(other)
    digits = x_in.reshape(16, 2 * CAP, 2, WIDE)[:, :2, :, D:].reshape(IMAGES, 128)
    g_in, digits = lax.optimization_barrier((g_in, digits))
    targets, class_weight = run(
        label_body,
        (shape((4, COLS), F32), shape((1, COLS), F32)),
        first_class,
        digits,
        labels,
        specs=[SMEM, VMEM, VMEM],
        name="labels",
        cost=LONG,
    )
    own, class_weight = lax.optimization_barrier((own, class_weight))
    out_in = chip_swap(add_cores(own, other, "add_out"))
    gs, d_pre, own, other = expert_kernel(
        backward_body, (g_in, core_swap(g_in), slope, w_in, w_out), 2, PACKED, "backward"
    )
    other = core_swap(other)
    mixed_out, d_combine, token_sum = run(
        mixed_body,
        (shape((TOK, D), BF16), shape((2, TOK), F32), shape((1, D), F32)),
        table,
        out_in,
        tokens,
        out_grad,
        combine,
        name="mixed",
        cost=LONG,
    )
    token_sum = lax.psum(token_sum, "core")
    own, token_sum = lax.optimization_barrier((own, token_sum))
    rows_send = add_cores(own, other, "add_rows")
    rows_send, *sums = lax.optimization_barrier((rows_send, *y_parts(token_sum)))
    rows_in = chip_swap(rows_send)
    pooled, part, dp_send = run(
        head_body,
        (shape((4, D), F32), shape((4, D + 128), F32), shape((16, 4, COLS + 128), BF16)),
        here,
        *sums,
        targets,
        class_weight,
        head_w,
        specs=[SMEM] + [VMEM] * 7,
        name="head",
    )
    hidden, part = lax.optimization_barrier((hidden, part))
    d_w_out = weight_grad(hidden, gs, "d_w_out")
    messages = y_parts(lax.psum(part, "core"))
    pooled, d_w_out = lax.optimization_barrier((pooled, d_w_out))
    d_pooled, losses = run(
        pooled_body,
        (shape((4, D), F32), shape((1, 4), F32)),
        here,
        *messages,
        pooled,
        specs=[SMEM] + [VMEM] * 5,
        name="d_pooled",
    )
    dp_send, rows_in, xs, d_pooled = lax.optimization_barrier((dp_send, rows_in, xs, d_pooled))
    dp_in = lax.all_to_all(dp_send, "dp", 0, 0, tiled=True).reshape(IMAGES, COLS + 128)
    d_tokens = run(tokens_body, shape((TOK, D), BF16), table, rows_in, out_grad, name="d_tokens")
    d_w_in = weight_grad(xs, d_pre, "d_w_in")
    d_head = dot(dp_in[:, COLS : COLS + 80], dp_in[:, :COLS], 0, 0).astype(BF16)
    return (mixed_out, d_tokens, d_combine.T, d_w_in, d_w_out, losses.reshape(4), d_pooled, d_head)


def solution(mesh):
    grid = Mesh(mesh.devices.reshape(16, 2, 2, 2), ALL)
    rows = P(ALL, None)
    in_specs = (rows, rows, rows, P(None, ALL), rows, rows, P(None, EX), P("dp", None))
    out_specs = (
        rows,
        rows,
        rows,
        P(None, ALL),
        rows,
        P("dp"),
        P("dp", None),
        P("dp", EX),
    )
    return jax.shard_map(shards, mesh=grid, in_specs=in_specs, out_specs=out_specs, check_vma=False)
```

```python
import math

import jax
import jax.numpy as jnp
from jax import lax
from jax.experimental import pallas as pl
from jax.experimental.pallas import tpu as pltpu
from jax.sharding import Mesh, PartitionSpec as P

D = 1280
EXPERTS = 32
PATCHES = 256
CLASSES = 17408
CAP = 10
CHIPS = 64
IMAGES = 64
TOK = 128
HALF = CHIPS * CAP
ROWS = 2 * HALF
COLS = CLASSES // 8
BETA = 0.99
LOG_BETA = math.log(BETA)
EPS = 1e-06

CHIP = ("dp", "yh", "yl")
Y = ("yh", "yl")
EX = ("yh", "yl", "core")
ALL = ("dp", "yh", "yl", "core")
SWAP = [(0, 1), (1, 0)]
F32 = jnp.float32
BF16 = jnp.bfloat16
I32 = jnp.int32
PACKED = (HALF // 2, 2, D)
WIDE = D + 128
PACKED_X = (HALF // 2, 2, WIDE)
ROOT_2_PI = 0.7978845608028654
CUBIC = 0.044715


def dot(a, b, ca, cb):
    return lax.dot_general(a, b, (((ca,), (cb,)), ((), ())), preferred_element_type=F32)


def shape(dims, dtype):
    return jax.ShapeDtypeStruct(dims, dtype)


VMEM = pl.BlockSpec(memory_space=pltpu.VMEM)
SMEM = pl.BlockSpec(memory_space=pltpu.SMEM)
ANY = pl.BlockSpec(memory_space=pl.ANY)


TINY = pl.CostEstimate(flops=1, transcendentals=0, bytes_accessed=1)


LONG = pl.CostEstimate(flops=1 << 34, transcendentals=0, bytes_accessed=1 << 26)


def run(body, outs, *args, grid=(), specs=None, out_specs=None, scratch=(), name=None, cost=TINY, limit=56):
    return pl.pallas_call(
        body,
        out_shape=outs,
        grid=grid,
        in_specs=specs or [VMEM] * len(args),
        out_specs=out_specs or jax.tree.map(lambda _: VMEM, outs),
        scratch_shapes=list(scratch),
        name=name,
        cost_estimate=cost,
        compiler_params=pltpu.CompilerParams(vmem_limit_bytes=limit << 20),
    )(*args)


def pack_rows(ref, value):
    ref[...] = value.astype(BF16).reshape(ref.shape)


def in_vmem(value):
    return pltpu.with_memory_space_constraint(value, pltpu.VMEM)


def x_body(routes_ref, labels_ref, tokens_ref, table_ref, send_ref):
    ids = lax.broadcasted_iota(I32, (EXPERTS, TOK), 0)
    routes = (routes_ref[0:1, :], routes_ref[1:2, :])
    hit = [r == ids for r in routes]
    hits = jnp.where(hit[0], 1.0, jnp.where(hit[1], 1.0, 0.0)).astype(BF16)
    t_row = lax.broadcasted_iota(I32, (TOK, TOK), 0)
    t_col = lax.broadcasted_iota(I32, (TOK, TOK), 1)
    before = jnp.where(t_row < t_col, 1.0, 0.0).astype(BF16)
    earlier = dot(hits, before, 1, 0)
    slot = lax.broadcasted_iota(I32, (HALF, TOK), 0)
    both = jnp.zeros((HALF, TOK), F32)
    for k in range(2):
        pos = jnp.sum(jnp.where(hit[k], earlier, 0.0), axis=0, keepdims=True)
        row = routes[k] * (2 * CAP) + pos.astype(I32)
        table = jnp.where(slot == row, 1.0, jnp.where(slot == row + CAP, 1.0, 0.0))
        table_ref[k] = table.astype(BF16)
        both = both + table
    rows = dot(both.astype(BF16), tokens_ref[...], 1, 0)
    labels = labels_ref[...]
    high = lax.shift_right_logical(labels, 8)
    low = labels - high * 256
    digits = jnp.concatenate(
        [high.astype(F32), low.astype(F32), jnp.zeros((4, 120), F32)], axis=1
    ).astype(BF16)
    place = lax.broadcasted_iota(I32, (HALF, 4), 0)
    image = lax.broadcasted_iota(I32, (HALF, 4), 1)
    chip = lax.shift_right_logical(place * 6554, 16)
    spread = jnp.where(place - CAP * chip == image, 1.0, 0.0).astype(BF16)
    pack_rows(send_ref, jnp.concatenate([rows, dot(spread, digits, 1, 0)], axis=1))


def g_body(table_ref, grad_ref, combine_ref, send_ref):
    table0, table1 = table_ref[0].astype(F32), table_ref[1].astype(F32)
    scale = jnp.sum(
        table0 * combine_ref[0:1, :] + table1 * combine_ref[1:2, :], axis=1, keepdims=True
    )
    pack_rows(send_ref, scale * dot((table0 + table1).astype(BF16), grad_ref[...], 1, 0))


HALVES = (slice(0, HALF), slice(HALF, ROWS))


def chunks(part, size):
    return [slice(n, n + size) for n in range(part.start, part.stop, size)]


def start_all(pairs, sems):
    copies = [pltpu.make_async_copy(s, d, sems.at[n]) for n, (s, d) in enumerate(pairs)]
    for copy in copies:
        copy.start()
    return copies


def forward_body(
    own_x, other_x, w1_in, w2_in, xs_out, hidden_out, slope_out, own_out, other_out,
    w1, w2, xs, hidden, slope, own, other, in_sems, out_sems,
):
    copies = start_all(((w1_in, w1), (w2_in, w2)), in_sems)
    saved = []
    for n, half in enumerate(HALVES):
        xs[half] = (own_x, other_x)[n][:, :, :D].reshape(HALF, D)
        if n == 0:
            copies[0].wait()
        for rows in chunks(half, 160):
            h = dot(xs[rows, :], w1[...], 1, 0)
            square = h * h
            bend = jnp.tanh(h * (ROOT_2_PI + (ROOT_2_PI * CUBIC) * square))
            act = 0.5 + 0.5 * bend
            hidden[rows, :] = (h * act).astype(BF16)
            tilt = (1.0 - bend * bend) * (0.5 * ROOT_2_PI + (1.5 * ROOT_2_PI * CUBIC) * square)
            slope[rows, :] = (act + h * tilt).astype(BF16)
        saved += start_all(
            [(v.at[half], o.at[half]) for v, o in ((xs, xs_out), (hidden, hidden_out), (slope, slope_out))],
            out_sems.at[n],
        )
        if n == 0:
            copies[1].wait()
        for rows in chunks(half, 160):
            part = dot(hidden[rows, :], w2[...], 1, 0)
            there = slice(rows.start - half.start, rows.stop - half.start)
            if n == 0:
                own[there, :] = part
            else:
                other[there, :] = part.astype(BF16)
        saved += start_all([((own, other)[n], (own_out, other_out)[n])], out_sems.at[2 + n])
    for copy in saved:
        copy.wait()


def backward_body(
    own_g, other_g, slope_in, w1_in, w2_in, gs_out, d_pre_out, own_out, other_out,
    slope, w1, w2, gs, d_pre, own, other, in_sems, out_sems,
):
    first, last = HALVES
    pairs = (
        (w2_in, w2), (slope_in.at[first], slope.at[first]), (w1_in, w1),
        (slope_in.at[last], slope.at[last]),
    )
    copies = start_all(pairs, in_sems)
    saved = []
    for n, half in enumerate(HALVES):
        gs[half] = (own_g, other_g)[n][...].reshape(HALF, D)
        if n == 0:
            copies[0].wait()
        copies[(1, 3)[n]].wait()
        for rows in chunks(half, 320):
            d_h = dot(gs[rows, :], w2[...], 1, 1)
            d_pre[rows, :] = (d_h * slope[rows, :].astype(F32)).astype(BF16)
        saved += start_all(
            [(v.at[half], o.at[half]) for v, o in ((gs, gs_out), (d_pre, d_pre_out))],
            out_sems.at[n],
        )
        if n == 0:
            copies[2].wait()
        for rows in chunks(half, 320):
            part = dot(d_pre[rows, :], w1[...], 1, 1)
            there = slice(rows.start - half.start, rows.stop - half.start)
            if n == 0:
                own[there, :] = part
            else:
                other[there, :] = part.astype(BF16)
        saved += start_all([((own, other)[n], (own_out, other_out)[n])], out_sems.at[2 + n])
    for copy in saved:
        copy.wait()


SQUARE = (ROWS, D)


def expert_kernel(body, ins, kept, name):
    outs = (*[shape(SQUARE, BF16)] * kept, shape((HALF, D), F32), shape((HALF, D), BF16))
    scratch = [pltpu.VMEM((D, D), BF16)] * (len(ins) - 2)
    scratch += [pltpu.VMEM(SQUARE, BF16)] * (kept if len(ins) == 4 else 2)
    scratch += [pltpu.VMEM((HALF, D), F32), pltpu.VMEM((HALF, D), BF16)]
    scratch += [
        pltpu.SemaphoreType.DMA((4,)),
        pltpu.SemaphoreType.DMA((4, 3)),
    ]
    return run(
        body,
        outs,
        in_vmem(ins[0]),
        in_vmem(ins[1]),
        *ins[2:],
        specs=[VMEM] * 2 + [ANY] * (len(ins) - 2),
        out_specs=tuple([ANY] * len(outs)),
        scratch=scratch,
        name=name,
    )


GRAD_COLS = 640


def weight_grad_body(left_ref, right_ref, out_ref):
    out_ref[...] = dot(left_ref[...], right_ref[...], 0, 0).astype(BF16)


def weight_grad(left, right, name):
    return run(
        weight_grad_body,
        shape((D, D), BF16),
        left,
        right,
        grid=(D // GRAD_COLS,),
        specs=[pl.BlockSpec((ROWS, GRAD_COLS), lambda i: (0, i)), pl.BlockSpec((ROWS, D), lambda i: (0, 0))],
        out_specs=pl.BlockSpec((GRAD_COLS, D), lambda i: (i, 0)),
        name=name,
    )


def mark_body(in_ref, out_ref):
    out_ref[0] = in_ref[0]


def add_body(own_ref, other_ref, send_ref):
    rows = pl.ds(pl.multiple_of(pl.program_id(0) * ADD_ROWS, ADD_ROWS), ADD_ROWS)
    pack_rows(send_ref, own_ref[...] + other_ref[rows, :].astype(F32))


ADD_ROWS = 320


def add_cores(own, other, name, cost=TINY):
    rows = pl.BlockSpec((ADD_ROWS, D), lambda i: (i, 0))
    return run(
        add_body,
        shape(PACKED, BF16),
        own,
        in_vmem(other),
        grid=(HALF // ADD_ROWS,),
        specs=[rows, VMEM],
        out_specs=pl.BlockSpec((ADD_ROWS // 2, 2, D), lambda i: (i, 0, 0)),
        name=name,
        cost=cost,
    )


def across(row):
    return jnp.sum(jnp.where(eye(), row, 0.0), axis=1, keepdims=True)


def along(column):
    return jnp.sum(jnp.where(eye(), column, 0.0), axis=0, keepdims=True)


def eye():
    return lax.broadcasted_iota(I32, (TOK, TOK), 0) == lax.broadcasted_iota(I32, (TOK, TOK), 1)


def mixed_body(table_ref, in_ref, tokens_ref, grad_ref, combine_ref, mixed_ref, dc_ref, sum_ref):
    rows = in_ref[...].reshape(HALF, D)
    vals0 = dot(table_ref[0], rows, 0, 0)
    vals1 = dot(table_ref[1], rows, 0, 0)
    grad = grad_ref[...].astype(F32)
    dc_ref[0:1, :] = along(jnp.sum(grad * vals0, axis=1, keepdims=True))
    dc_ref[1:2, :] = along(jnp.sum(grad * vals1, axis=1, keepdims=True))
    mixed = (
        tokens_ref[...].astype(F32)
        + (across(combine_ref[0:1, :]) * vals0 + across(combine_ref[1:2, :]) * vals1)
    ).astype(BF16)
    mixed_ref[...] = mixed
    sum_ref[...] = jnp.sum(mixed.astype(F32), axis=0, keepdims=True)


def tokens_body(table_ref, in_ref, grad_ref, out_ref):
    rows = in_ref[...].reshape(HALF, D)
    table = (table_ref[0].astype(F32) + table_ref[1].astype(F32)).astype(BF16)
    out_ref[...] = (grad_ref[...].astype(F32) + dot(table, rows, 0, 0)).astype(BF16)


def in_order(here, parts, j):
    pick = parts[0]
    for shift in (1, 2, 3):
        pick = jnp.where((here + shift) % 4 == j, parts[shift], pick)
    return pick


def y_parts(mine):
    return [in_vmem(mine)] + [
        in_vmem(lax.ppermute(mine, Y, [((i + shift) % 4, i) for i in range(4)]))
        for shift in (1, 2, 3)
    ]


def centered(pooled):
    away = pooled - jnp.mean(pooled, axis=1, keepdims=True)
    return away, lax.rsqrt(jnp.mean(away * away, axis=1, keepdims=True) + EPS)


def head_body(here_ref, p0, p1, p2, p3, target_ref, weight_ref, w_ref, pooled_ref, part_ref, send_ref):
    here = here_ref[0]
    parts = [p[...] for p in (p0, p1, p2, p3)]
    for j in range(4):
        pooled_ref[j : j + 1, :] = in_order(here, parts, j) * (1.0 / PATCHES)
    away, scale = centered(pooled_ref[...])
    normed = (away * scale).astype(BF16)
    logits = dot(normed, w_ref[...], 1, 0)
    hit = target_ref[...] > 0.5
    signed = jnp.where(hit, -logits, logits)
    small = jnp.exp(-jnp.abs(signed))
    nll = jnp.maximum(signed, 0.0) + jnp.log1p(small)
    inverse = 1.0 / (1.0 + small)
    miss = jnp.where(signed >= 0.0, 1.0, small) * inverse
    keep = jnp.where(signed >= 0.0, small, 1.0) * inverse
    weight = weight_ref[...]
    loss = jnp.sum(weight * (miss * miss) * nll, axis=1, keepdims=True)
    slope = weight * (2.0 * miss * keep * nll + miss * miss) * miss
    d_logits = jnp.where(hit, -slope, slope).astype(BF16)
    part_ref[:, :D] = dot(d_logits, w_ref[...], 1, 1)
    part_ref[:, D:] = jnp.broadcast_to(loss, (4, 128))
    zeros = jnp.zeros((4, 48), BF16)
    for d in range(16):
        send_ref[d, :, :COLS] = d_logits
        send_ref[d, :, COLS : COLS + 128] = jnp.concatenate(
            [normed[:, 80 * d : 80 * d + 80], zeros], axis=1
        )


def pooled_body(here_ref, m0, m1, m2, m3, pooled_ref, d_ref, loss_ref):
    here = here_ref[0]
    parts = [m[...] for m in (m0, m1, m2, m3)]
    total = in_order(here, parts, 0)
    for j in (1, 2, 3):
        total = total + in_order(here, parts, j)
    away, scale = centered(pooled_ref[...])
    normed = away * scale
    d_normed = total[:, :D]
    mean = jnp.mean(d_normed, axis=1, keepdims=True)
    along = jnp.mean(d_normed * normed, axis=1, keepdims=True)
    d_ref[...] = scale * (d_normed - mean - normed * along)
    diagonal = lax.broadcasted_iota(I32, (4, 4), 0) == lax.broadcasted_iota(I32, (4, 4), 1)
    loss_ref[...] = jnp.sum(
        jnp.where(diagonal, total[:, D : D + 1], 0.0), axis=0, keepdims=True
    )


def effective_of(counts):
    return (1.0 - BETA) / (1.0 - jnp.exp((counts + 1.0) * LOG_BETA))


def label_body(first_ref, digits_ref, labels_ref, target_ref, weight_ref):
    ids = (lax.broadcasted_iota(I32, (1, COLS), 1) + first_ref[0]).astype(F32)
    own = labels_ref[...].astype(F32)
    target = own[:, 0:1] == ids
    for n in range(1, 4):
        target = target | (own[:, n : n + 1] == ids)
    target_ref[...] = jnp.where(target, 1.0, 0.0)
    digits = digits_ref[...].astype(F32)
    labels = digits[:, 0:4] * 256.0 + digits[:, 4:8]
    padded = jnp.concatenate([labels, jnp.zeros((IMAGES, 124), F32)], axis=1)
    turned = jnp.concatenate([padded, jnp.zeros((128 - IMAGES, 128), F32)], axis=0).T
    columns = [labels[:, n : n + 1] for n in range(4)]
    rows = [turned[n : n + 1, :IMAGES] for n in range(4)]

    def fresh_of(entries):
        out = [jnp.ones_like(entries[0])]
        for n in range(1, 4):
            keep = out[0]
            for m in range(n):
                keep = jnp.where(entries[m] == entries[n], 0.0, keep)
            out.append(keep)
        return out

    fresh, fresh_row = fresh_of(columns), fresh_of(rows)
    counts = jnp.zeros((IMAGES, COLS), F32)
    excess = jnp.zeros((IMAGES, 1), F32)
    base = effective_of(jnp.zeros((IMAGES, 1), F32))
    for n in range(4):
        counts = counts + jnp.where(columns[n] == ids, fresh[n], 0.0)
        same = jnp.zeros((IMAGES, IMAGES), F32)
        for m in range(4):
            same = same + jnp.where(columns[n] == rows[m], fresh_row[m], 0.0)
        count = jnp.sum(same, axis=1, keepdims=True)
        excess = excess + fresh[n] * (effective_of(count) - base) / count
    total = CLASSES * base[0:1, :] + jnp.sum(excess, axis=0, keepdims=True)
    weight_ref[...] = effective_of(jnp.sum(counts, axis=0, keepdims=True)) * (CLASSES / total)


def chip_swap(packed):
    dims = packed.shape
    blocks = packed.reshape(CHIPS, CAP // 2, 2, dims[-1])
    return lax.all_to_all(blocks, CHIP, 0, 0, tiled=True).reshape(dims)


def core_swap(rows):
    return lax.ppermute(rows, "core", SWAP)


def shards(tokens, routes, combine, w_in, w_out, out_grad, head_w, labels):
    here = lax.axis_index(Y).astype(I32).reshape(1)
    first_class = (lax.axis_index(EX) * COLS).astype(I32).reshape(1)
    combine = combine.T
    table, x_send = run(
        x_body,
        (shape((2, HALF, TOK), BF16), shape(PACKED_X, BF16)),
        routes.T,
        labels,
        tokens,
        name="dispatch_x",
    )
    x_in = chip_swap(x_send)
    g_send = run(g_body, shape(PACKED, BF16), table, out_grad, combine, name="dispatch_g")
    x_in, g_send = lax.optimization_barrier((x_in, g_send))
    g_in = chip_swap(g_send)
    xs, hidden, slope, own, other = expert_kernel(
        forward_body, (x_in, core_swap(x_in), w_in, w_out), 3, "forward"
    )
    other = core_swap(other)
    digits = x_in.reshape(16, 2 * CAP, 2, WIDE)[:, :2, :, D:].reshape(IMAGES, 128)
    targets, class_weight = run(
        label_body,
        (shape((4, COLS), F32), shape((1, COLS), F32)),
        first_class,
        digits,
        labels,
        specs=[SMEM, VMEM, VMEM],
        name="labels",
    )
    g_in, mark = lax.optimization_barrier((g_in, here))
    mark = run(mark_body, shape((1,), I32), mark, specs=[SMEM], out_specs=SMEM, name="mark", cost=LONG)
    own, mark = lax.optimization_barrier((own, mark))
    out_in = chip_swap(add_cores(own, other, "add_out"))
    gs, d_pre, own, other = expert_kernel(
        backward_body, (g_in, core_swap(g_in), slope, w_in, w_out), 2, "backward"
    )
    other = core_swap(other)
    d_w_out = weight_grad(hidden, gs, "d_w_out")
    out_in, d_w_out, targets, class_weight = lax.optimization_barrier(
        (out_in, d_w_out, targets, class_weight)
    )
    mixed_out, d_combine, token_sum = run(
        mixed_body,
        (shape((TOK, D), BF16), shape((2, TOK), F32), shape((1, D), F32)),
        table,
        in_vmem(out_in),
        tokens,
        out_grad,
        combine,
        name="mixed",
        cost=LONG,
    )
    token_sum = lax.psum(token_sum, "core")
    own, token_sum = lax.optimization_barrier((own, token_sum))
    rows_send = add_cores(own, other, "add_rows")
    rows_send, *sums = lax.optimization_barrier((rows_send, *y_parts(token_sum)))
    rows_in = chip_swap(rows_send)
    pooled, part, dp_send = run(
        head_body,
        (shape((4, D), F32), shape((4, D + 128), F32), shape((16, 4, COLS + 128), BF16)),
        here,
        *sums,
        targets,
        class_weight,
        head_w,
        specs=[SMEM] + [VMEM] * 7,
        name="head",
    )
    xs, part = lax.optimization_barrier((xs, part))
    messages = y_parts(lax.psum(part, "core"))
    d_w_in = weight_grad(xs, d_pre, "d_w_in")
    pooled, d_w_in = lax.optimization_barrier((pooled, d_w_in))
    d_pooled, losses = run(
        pooled_body,
        (shape((4, D), F32), shape((1, 4), F32)),
        here,
        *messages,
        pooled,
        specs=[SMEM] + [VMEM] * 5,
        name="d_pooled",
    )
    dp_send, rows_in, d_pooled = lax.optimization_barrier((dp_send, rows_in, d_pooled))
    dp_in = lax.all_to_all(dp_send, "dp", 0, 0, tiled=True).reshape(IMAGES, COLS + 128)
    d_tokens = run(tokens_body, shape((TOK, D), BF16), table, in_vmem(rows_in), out_grad, name="d_tokens")
    d_head = dot(dp_in[:, COLS : COLS + 80], dp_in[:, :COLS], 0, 0).astype(BF16)
    return (mixed_out, d_tokens, d_combine.T, d_w_in, d_w_out, losses.reshape(4), d_pooled, d_head)


def solution(mesh):
    grid = Mesh(mesh.devices.reshape(16, 2, 2, 2), ALL)
    rows = P(ALL, None)
    in_specs = (rows, rows, rows, P(None, ALL), rows, rows, P(None, EX), P("dp", None))
    out_specs = (
        rows,
        rows,
        rows,
        P(None, ALL),
        rows,
        P("dp"),
        P("dp", None),
        P("dp", EX),
    )
    return jax.shard_map(shards, mesh=grid, in_specs=in_specs, out_specs=out_specs, check_vma=False)
```

```python
import math

import jax
import jax.numpy as jnp
from jax import lax
from jax.experimental import pallas as pl
from jax.experimental.pallas import tpu as pltpu
from jax.sharding import Mesh, PartitionSpec as P

D = 1280
EXPERTS = 32
PATCHES = 256
CLASSES = 17408
CAP = 10
CHIPS = 64
IMAGES = 64
TOK = 128
HALF = CHIPS * CAP
ROWS = 2 * HALF
COLS = CLASSES // 8
BETA = 0.99
LOG_BETA = math.log(BETA)
EPS = 1e-06

CHIP = ("dp", "yh", "yl")
Y = ("yh", "yl")
EX = ("yh", "yl", "core")
ALL = ("dp", "yh", "yl", "core")
SWAP = [(0, 1), (1, 0)]
F32 = jnp.float32
BF16 = jnp.bfloat16
I32 = jnp.int32
PACKED = (HALF // 2, 2, D)
WIDE = D + 128
PACKED_X = (HALF // 2, 2, WIDE)
ROOT_2_PI = 0.7978845608028654
CUBIC = 0.044715


def dot(a, b, ca, cb):
    return lax.dot_general(a, b, (((ca,), (cb,)), ((), ())), preferred_element_type=F32)


def shape(dims, dtype):
    return jax.ShapeDtypeStruct(dims, dtype)


VMEM = pl.BlockSpec(memory_space=pltpu.VMEM)
SMEM = pl.BlockSpec(memory_space=pltpu.SMEM)
ANY = pl.BlockSpec(memory_space=pl.ANY)


TINY = pl.CostEstimate(flops=1, transcendentals=0, bytes_accessed=1)


LONG = pl.CostEstimate(flops=1 << 34, transcendentals=0, bytes_accessed=1 << 26)


def run(body, outs, *args, grid=(), specs=None, out_specs=None, scratch=(), name=None, cost=TINY, limit=56):
    return pl.pallas_call(
        body,
        out_shape=outs,
        grid=grid,
        in_specs=specs or [VMEM] * len(args),
        out_specs=out_specs or jax.tree.map(lambda _: VMEM, outs),
        scratch_shapes=list(scratch),
        name=name,
        cost_estimate=cost,
        compiler_params=pltpu.CompilerParams(vmem_limit_bytes=limit << 20),
    )(*args)


def pack_rows(ref, value):
    ref[...] = value.astype(BF16).reshape(ref.shape)


def in_vmem(value):
    return pltpu.with_memory_space_constraint(value, pltpu.VMEM)


def x_body(routes_ref, labels_ref, tokens_ref, table_ref, send_ref):
    ids = lax.broadcasted_iota(I32, (EXPERTS, TOK), 0)
    routes = (routes_ref[0:1, :], routes_ref[1:2, :])
    hit = [r == ids for r in routes]
    hits = jnp.where(hit[0], 1.0, jnp.where(hit[1], 1.0, 0.0)).astype(BF16)
    t_row = lax.broadcasted_iota(I32, (TOK, TOK), 0)
    t_col = lax.broadcasted_iota(I32, (TOK, TOK), 1)
    before = jnp.where(t_row < t_col, 1.0, 0.0).astype(BF16)
    earlier = dot(hits, before, 1, 0)
    slot = lax.broadcasted_iota(I32, (HALF, TOK), 0)
    both = jnp.zeros((HALF, TOK), F32)
    for k in range(2):
        pos = jnp.sum(jnp.where(hit[k], earlier, 0.0), axis=0, keepdims=True)
        row = routes[k] * (2 * CAP) + pos.astype(I32)
        table = jnp.where(slot == row, 1.0, jnp.where(slot == row + CAP, 1.0, 0.0))
        table_ref[k] = table.astype(BF16)
        both = both + table
    rows = dot(both.astype(BF16), tokens_ref[...], 1, 0)
    labels = labels_ref[...]
    high = lax.shift_right_logical(labels, 8)
    low = labels - high * 256
    digits = jnp.concatenate(
        [high.astype(F32), low.astype(F32), jnp.zeros((4, 120), F32)], axis=1
    ).astype(BF16)
    place = lax.broadcasted_iota(I32, (HALF, 4), 0)
    image = lax.broadcasted_iota(I32, (HALF, 4), 1)
    chip = lax.shift_right_logical(place * 6554, 16)
    spread = jnp.where(place - CAP * chip == image, 1.0, 0.0).astype(BF16)
    pack_rows(send_ref, jnp.concatenate([rows, dot(spread, digits, 1, 0)], axis=1))


def g_body(table_ref, grad_ref, combine_ref, send_ref):
    table0, table1 = table_ref[0].astype(F32), table_ref[1].astype(F32)
    scale = jnp.sum(
        table0 * combine_ref[0:1, :] + table1 * combine_ref[1:2, :], axis=1, keepdims=True
    )
    pack_rows(send_ref, scale * dot((table0 + table1).astype(BF16), grad_ref[...], 1, 0))


HALVES = (slice(0, HALF), slice(HALF, ROWS))


def chunks(part, size):
    return [slice(n, n + size) for n in range(part.start, part.stop, size)]


def start_all(pairs, sems):
    copies = [pltpu.make_async_copy(s, d, sems.at[n]) for n, (s, d) in enumerate(pairs)]
    for copy in copies:
        copy.start()
    return copies


def forward_body(
    own_x, other_x, w1_in, w2_in, xs_out, hidden_out, slope_out, own_out, other_out,
    w1, w2, xs, hidden, slope, own, other, in_sems, out_sems,
):
    copies = start_all(((w1_in, w1), (w2_in, w2)), in_sems)
    saved = []
    for n, half in enumerate(HALVES):
        xs[half] = (own_x, other_x)[n][:, :, :D].reshape(HALF, D)
        if n == 0:
            copies[0].wait()

        def activate(i, carry):
            for low in (0, 160):
                rows = pl.ds(pl.multiple_of(half.start + low + i * 320, 160), 160)
                h = dot(xs[rows, :], w1[...], 1, 0)
                square = h * h
                bend = jnp.tanh(h * (ROOT_2_PI + (ROOT_2_PI * CUBIC) * square))
                act = 0.5 + 0.5 * bend
                hidden[rows, :] = (h * act).astype(BF16)
                tilt = (1.0 - bend * bend) * (
                    0.5 * ROOT_2_PI + (1.5 * ROOT_2_PI * CUBIC) * square
                )
                slope[rows, :] = (act + h * tilt).astype(BF16)
            return carry

        lax.fori_loop(0, 2, activate, 0)
        saved += start_all(
            [(v.at[half], o.at[half]) for v, o in ((xs, xs_out), (hidden, hidden_out), (slope, slope_out))],
            out_sems.at[n],
        )
        if n == 0:
            copies[1].wait()
        for rows in chunks(half, 160):
            part = dot(hidden[rows, :], w2[...], 1, 0)
            there = slice(rows.start - half.start, rows.stop - half.start)
            if n == 0:
                own[there, :] = part
            else:
                other[there, :] = part.astype(BF16)
        saved += start_all([((own, other)[n], (own_out, other_out)[n])], out_sems.at[2 + n])
    for copy in saved:
        copy.wait()


def backward_body(
    own_g, other_g, slope_in, w1_in, w2_in, gs_out, d_pre_out, own_out, other_out,
    slope, w1, w2, gs, d_pre, own, other, in_sems, out_sems,
):
    first, last = HALVES
    pairs = (
        (w2_in, w2), (slope_in.at[first], slope.at[first]), (w1_in, w1),
        (slope_in.at[last], slope.at[last]),
    )
    copies = start_all(pairs, in_sems)
    saved = []
    for n, half in enumerate(HALVES):
        gs[half] = (own_g, other_g)[n][...].reshape(HALF, D)
        if n == 0:
            copies[0].wait()
        copies[(1, 3)[n]].wait()
        for rows in chunks(half, 320):
            d_h = dot(gs[rows, :], w2[...], 1, 1)
            d_pre[rows, :] = (d_h * slope[rows, :].astype(F32)).astype(BF16)
        saved += start_all(
            [(v.at[half], o.at[half]) for v, o in ((gs, gs_out), (d_pre, d_pre_out))],
            out_sems.at[n],
        )
        if n == 0:
            copies[2].wait()
        for rows in chunks(half, 320):
            part = dot(d_pre[rows, :], w1[...], 1, 1)
            there = slice(rows.start - half.start, rows.stop - half.start)
            if n == 0:
                own[there, :] = part
            else:
                other[there, :] = part.astype(BF16)
        saved += start_all([((own, other)[n], (own_out, other_out)[n])], out_sems.at[2 + n])
    for copy in saved:
        copy.wait()


SQUARE = (ROWS, D)


def expert_kernel(body, ins, kept, name):
    outs = (*[shape(SQUARE, BF16)] * kept, shape((HALF, D), F32), shape((HALF, D), BF16))
    scratch = [pltpu.VMEM((D, D), BF16)] * (len(ins) - 2)
    scratch += [pltpu.VMEM(SQUARE, BF16)] * (kept if len(ins) == 4 else 2)
    scratch += [pltpu.VMEM((HALF, D), F32), pltpu.VMEM((HALF, D), BF16)]
    scratch += [
        pltpu.SemaphoreType.DMA((4,)),
        pltpu.SemaphoreType.DMA((4, 3)),
    ]
    return run(
        body,
        outs,
        in_vmem(ins[0]),
        in_vmem(ins[1]),
        *ins[2:],
        specs=[VMEM] * 2 + [ANY] * (len(ins) - 2),
        out_specs=tuple([ANY] * len(outs)),
        scratch=scratch,
        name=name,
    )


GRAD_COLS = 640


def weight_grad_body(left_ref, right_ref, *refs):
    refs[-1][...] = dot(left_ref[...], right_ref[...], 0, 0).astype(BF16)


def weight_grad(left, right, name, blocks=(0, 1), into=()):
    first = blocks[0]
    return pl.pallas_call(
        weight_grad_body,
        out_shape=shape((D, D), BF16),
        grid=(len(blocks),),
        in_specs=[
            pl.BlockSpec((ROWS, GRAD_COLS), lambda i: (0, first + i)),
            pl.BlockSpec((ROWS, D), lambda i: (0, 0)),
            *[ANY for _ in into],
        ],
        out_specs=pl.BlockSpec((GRAD_COLS, D), lambda i: (first + i, 0)),
        input_output_aliases={2: 0} if into else {},
        name=name,
        cost_estimate=TINY,
        compiler_params=pltpu.CompilerParams(vmem_limit_bytes=56 << 20),
    )(left, right, *into)


def mark_body(in_ref, out_ref):
    out_ref[0] = in_ref[0]


def add_body(own_ref, other_ref, send_ref):
    rows = pl.ds(pl.multiple_of(pl.program_id(0) * ADD_ROWS, ADD_ROWS), ADD_ROWS)
    pack_rows(send_ref, own_ref[...] + other_ref[rows, :].astype(F32))


ADD_ROWS = 320


def add_cores(own, other, name, cost=TINY):
    rows = pl.BlockSpec((ADD_ROWS, D), lambda i: (i, 0))
    return run(
        add_body,
        shape(PACKED, BF16),
        own,
        in_vmem(other),
        grid=(HALF // ADD_ROWS,),
        specs=[rows, VMEM],
        out_specs=pl.BlockSpec((ADD_ROWS // 2, 2, D), lambda i: (i, 0, 0)),
        name=name,
        cost=cost,
    )


def across(row):
    return jnp.sum(jnp.where(eye(), row, 0.0), axis=1, keepdims=True)


def along(column):
    return jnp.sum(jnp.where(eye(), column, 0.0), axis=0, keepdims=True)


def eye():
    return lax.broadcasted_iota(I32, (TOK, TOK), 0) == lax.broadcasted_iota(I32, (TOK, TOK), 1)


def mixed_body(table_ref, in_ref, tokens_ref, grad_ref, combine_ref, mixed_ref, dc_ref, sum_ref):
    rows = in_ref[...].reshape(HALF, D)
    vals0 = dot(table_ref[0], rows, 0, 0)
    vals1 = dot(table_ref[1], rows, 0, 0)
    grad = grad_ref[...].astype(F32)
    dc_ref[0:1, :] = along(jnp.sum(grad * vals0, axis=1, keepdims=True))
    dc_ref[1:2, :] = along(jnp.sum(grad * vals1, axis=1, keepdims=True))
    mixed = (
        tokens_ref[...].astype(F32)
        + (across(combine_ref[0:1, :]) * vals0 + across(combine_ref[1:2, :]) * vals1)
    ).astype(BF16)
    mixed_ref[...] = mixed
    sum_ref[...] = jnp.sum(mixed.astype(F32), axis=0, keepdims=True)


def tokens_body(table_ref, in_ref, grad_ref, out_ref):
    rows = in_ref[...].reshape(HALF, D)
    table = (table_ref[0].astype(F32) + table_ref[1].astype(F32)).astype(BF16)
    out_ref[...] = (grad_ref[...].astype(F32) + dot(table, rows, 0, 0)).astype(BF16)


def in_order(here, parts, j):
    pick = parts[0]
    for shift in (1, 2, 3):
        pick = jnp.where((here + shift) % 4 == j, parts[shift], pick)
    return pick


def y_parts(mine):
    return [in_vmem(mine)] + [
        in_vmem(lax.ppermute(mine, Y, [((i + shift) % 4, i) for i in range(4)]))
        for shift in (1, 2, 3)
    ]


def centered(pooled):
    away = pooled - jnp.mean(pooled, axis=1, keepdims=True)
    return away, lax.rsqrt(jnp.mean(away * away, axis=1, keepdims=True) + EPS)


CLASS_CUTS = (0, 640, 1152, 1664, COLS)


def head_body(
    here_ref, p0, p1, p2, p3, target_ref, weight_ref, w_in, pooled_ref, part_ref, send_ref, w_ref, sems
):
    spans = [slice(low, high) for low, high in zip(CLASS_CUTS, CLASS_CUTS[1:])]
    copies = start_all([(w_in.at[:, span], w_ref.at[:, span]) for span in spans], sems)
    here = here_ref[0]
    parts = [p[...] for p in (p0, p1, p2, p3)]
    for j in range(4):
        pooled_ref[j : j + 1, :] = in_order(here, parts, j) * (1.0 / PATCHES)
    away, scale = centered(pooled_ref[...])
    normed = (away * scale).astype(BF16)
    zeros = jnp.zeros((4, 48), BF16)
    for d in range(16):
        send_ref[d, :, COLS : COLS + 128] = jnp.concatenate(
            [normed[:, 80 * d : 80 * d + 80], zeros], axis=1
        )
    loss = jnp.zeros((4, 1), F32)
    d_normed = jnp.zeros((4, D), F32)
    for span, copy in zip(spans, copies):
        copy.wait()
        logits = dot(normed, w_ref[:, span], 1, 0)
        hit = target_ref[:, span] > 0.5
        signed = jnp.where(hit, -logits, logits)
        small = jnp.exp(-jnp.abs(signed))
        nll = jnp.maximum(signed, 0.0) + jnp.log1p(small)
        inverse = 1.0 / (1.0 + small)
        miss = jnp.where(signed >= 0.0, 1.0, small) * inverse
        keep = jnp.where(signed >= 0.0, small, 1.0) * inverse
        weight = weight_ref[:, span]
        loss = loss + jnp.sum(weight * (miss * miss) * nll, axis=1, keepdims=True)
        slope = weight * (2.0 * miss * keep * nll + miss * miss) * miss
        d_logits = jnp.where(hit, -slope, slope).astype(BF16)
        d_normed = d_normed + dot(d_logits, w_ref[:, span], 1, 1)
        for d in range(16):
            send_ref[d, :, span] = d_logits
    part_ref[:, :D] = d_normed
    part_ref[:, D:] = jnp.broadcast_to(loss, (4, 128))


def pooled_body(here_ref, m0, m1, m2, m3, pooled_ref, d_ref, loss_ref):
    here = here_ref[0]
    parts = [m[...] for m in (m0, m1, m2, m3)]
    total = in_order(here, parts, 0)
    for j in (1, 2, 3):
        total = total + in_order(here, parts, j)
    away, scale = centered(pooled_ref[...])
    normed = away * scale
    d_normed = total[:, :D]
    mean = jnp.mean(d_normed, axis=1, keepdims=True)
    along = jnp.mean(d_normed * normed, axis=1, keepdims=True)
    d_ref[...] = scale * (d_normed - mean - normed * along)
    diagonal = lax.broadcasted_iota(I32, (4, 4), 0) == lax.broadcasted_iota(I32, (4, 4), 1)
    loss_ref[...] = jnp.sum(
        jnp.where(diagonal, total[:, D : D + 1], 0.0), axis=0, keepdims=True
    )


def effective_of(counts):
    return (1.0 - BETA) / (1.0 - jnp.exp((counts + 1.0) * LOG_BETA))


def label_body(first_ref, digits_ref, labels_ref, target_ref, weight_ref):
    ids = (lax.broadcasted_iota(I32, (1, COLS), 1) + first_ref[0]).astype(F32)
    own = labels_ref[...].astype(F32)
    target = own[:, 0:1] == ids
    for n in range(1, 4):
        target = target | (own[:, n : n + 1] == ids)
    target_ref[...] = jnp.where(target, 1.0, 0.0)
    digits = digits_ref[...].astype(F32)
    labels = digits[:, 0:4] * 256.0 + digits[:, 4:8]
    padded = jnp.concatenate([labels, jnp.zeros((IMAGES, 124), F32)], axis=1)
    turned = jnp.concatenate([padded, jnp.zeros((128 - IMAGES, 128), F32)], axis=0).T
    columns = [labels[:, n : n + 1] for n in range(4)]
    rows = [turned[n : n + 1, :IMAGES] for n in range(4)]

    def fresh_of(entries):
        out = [jnp.ones_like(entries[0])]
        for n in range(1, 4):
            keep = out[0]
            for m in range(n):
                keep = jnp.where(entries[m] == entries[n], 0.0, keep)
            out.append(keep)
        return out

    fresh, fresh_row = fresh_of(columns), fresh_of(rows)
    counts = jnp.zeros((IMAGES, COLS), F32)
    excess = jnp.zeros((IMAGES, 1), F32)
    base = effective_of(jnp.zeros((IMAGES, 1), F32))
    for n in range(4):
        counts = counts + jnp.where(columns[n] == ids, fresh[n], 0.0)
        same = jnp.zeros((IMAGES, IMAGES), F32)
        for m in range(4):
            same = same + jnp.where(columns[n] == rows[m], fresh_row[m], 0.0)
        count = jnp.sum(same, axis=1, keepdims=True)
        excess = excess + fresh[n] * (effective_of(count) - base) / count
    total = CLASSES * base[0:1, :] + jnp.sum(excess, axis=0, keepdims=True)
    weight_ref[...] = effective_of(jnp.sum(counts, axis=0, keepdims=True)) * (CLASSES / total)


def chip_swap(packed):
    dims = packed.shape
    blocks = packed.reshape(CHIPS, CAP // 2, 2, dims[-1])
    return lax.all_to_all(blocks, CHIP, 0, 0, tiled=True).reshape(dims)


def core_swap(rows):
    return lax.ppermute(rows, "core", SWAP)


def shards(tokens, routes, combine, w_in, w_out, out_grad, head_w, labels):
    here = lax.axis_index(Y).astype(I32).reshape(1)
    first_class = (lax.axis_index(EX) * COLS).astype(I32).reshape(1)
    combine = combine.T
    table, x_send = run(
        x_body,
        (shape((2, HALF, TOK), BF16), shape(PACKED_X, BF16)),
        routes.T,
        labels,
        tokens,
        name="dispatch_x",
    )
    x_in = chip_swap(x_send)
    g_send = run(g_body, shape(PACKED, BF16), table, out_grad, combine, name="dispatch_g")
    x_in, g_send = lax.optimization_barrier((x_in, g_send))
    g_in = chip_swap(g_send)
    xs, hidden, slope, own, other = expert_kernel(
        forward_body, (x_in, core_swap(x_in), w_in, w_out), 3, "forward"
    )
    other = core_swap(other)
    digits = x_in.reshape(16, 2 * CAP, 2, WIDE)[:, :2, :, D:].reshape(IMAGES, 128)
    targets, class_weight = run(
        label_body,
        (shape((4, COLS), F32), shape((1, COLS), F32)),
        first_class,
        digits,
        labels,
        specs=[SMEM, VMEM, VMEM],
        name="labels",
    )
    g_in, targets, class_weight, mark = lax.optimization_barrier(
        (g_in, targets, class_weight, here)
    )
    mark = run(mark_body, shape((1,), I32), mark, specs=[SMEM], out_specs=SMEM, name="mark", cost=LONG)
    own, mark = lax.optimization_barrier((own, mark))
    out_in = chip_swap(add_cores(own, other, "add_out"))
    gs, d_pre, own, other = expert_kernel(
        backward_body, (g_in, core_swap(g_in), slope, w_in, w_out), 2, "backward"
    )
    other = core_swap(other)
    d_w_out = weight_grad(hidden, gs, "d_w_out")
    out_in, d_w_out = lax.optimization_barrier((out_in, d_w_out))
    mixed_out, d_combine, token_sum = run(
        mixed_body,
        (shape((TOK, D), BF16), shape((2, TOK), F32), shape((1, D), F32)),
        table,
        in_vmem(out_in),
        tokens,
        out_grad,
        combine,
        name="mixed",
        cost=LONG,
    )
    token_sum = lax.psum(token_sum, "core")
    own, token_sum = lax.optimization_barrier((own, token_sum))
    rows_send = add_cores(own, other, "add_rows")
    rows_send, *sums = lax.optimization_barrier((rows_send, *y_parts(token_sum)))
    rows_in = chip_swap(rows_send)
    pooled, part, dp_send = run(
        head_body,
        (shape((4, D), F32), shape((4, D + 128), F32), shape((16, 4, COLS + 128), BF16)),
        here,
        *sums,
        targets,
        class_weight,
        head_w,
        specs=[SMEM] + [VMEM] * 6 + [ANY],
        scratch=[pltpu.VMEM((D, COLS), BF16), pltpu.SemaphoreType.DMA((4,))],
        name="head",
    )
    xs, part = lax.optimization_barrier((xs, part))
    messages = y_parts(lax.psum(part, "core"))
    d_w_in = weight_grad(xs, d_pre, "d_w_in_low", blocks=(0,))
    pooled, d_w_in = lax.optimization_barrier((pooled, d_w_in))
    d_pooled, losses = run(
        pooled_body,
        (shape((4, D), F32), shape((1, 4), F32)),
        here,
        *messages,
        pooled,
        specs=[SMEM] + [VMEM] * 5,
        name="d_pooled",
    )
    dp_send, rows_in, d_pooled, d_w_in = lax.optimization_barrier(
        (dp_send, rows_in, d_pooled, d_w_in)
    )
    dp_in = lax.all_to_all(dp_send, "dp", 0, 0, tiled=True).reshape(IMAGES, COLS + 128)
    d_tokens = run(tokens_body, shape((TOK, D), BF16), table, in_vmem(rows_in), out_grad, name="d_tokens")
    d_w_in = weight_grad(xs, d_pre, "d_w_in_high", blocks=(1,), into=(d_w_in,))
    d_head = dot(dp_in[:, COLS : COLS + 80], dp_in[:, :COLS], 0, 0).astype(BF16)
    return (mixed_out, d_tokens, d_combine.T, d_w_in, d_w_out, losses.reshape(4), d_pooled, d_head)


def solution(mesh):
    grid = Mesh(mesh.devices.reshape(16, 2, 2, 2), ALL)
    rows = P(ALL, None)
    in_specs = (rows, rows, rows, P(None, ALL), rows, rows, P(None, EX), P("dp", None))
    out_specs = (
        rows,
        rows,
        rows,
        P(None, ALL),
        rows,
        P("dp"),
        P("dp", None),
        P("dp", EX),
    )
    return jax.shard_map(shards, mesh=grid, in_specs=in_specs, out_specs=out_specs, check_vma=False)
```

```python
import math

import jax
import jax.numpy as jnp
from jax import lax
from jax.experimental import pallas as pl
from jax.experimental.pallas import tpu as pltpu
from jax.sharding import Mesh, PartitionSpec as P

D = 1280
EXPERTS = 32
PATCHES = 256
CLASSES = 17408
CAP = 10
CHIPS = 64
IMAGES = 64
TOK = 128
HALF = CHIPS * CAP
ROWS = 2 * HALF
COLS = CLASSES // 8
BETA = 0.99
LOG_BETA = math.log(BETA)
EPS = 1e-06

CHIP = ("dp", "yh", "yl")
Y = ("yh", "yl")
EX = ("yh", "yl", "core")
ALL = ("dp", "yh", "yl", "core")
SWAP = [(0, 1), (1, 0)]
F32 = jnp.float32
BF16 = jnp.bfloat16
I32 = jnp.int32
PACKED = (HALF // 2, 2, D)
WIDE = D + 128
PACKED_X = (HALF // 2, 2, WIDE)
ROOT_2_PI = 0.7978845608028654
CUBIC = 0.044715


def dot(a, b, ca, cb):
    return lax.dot_general(a, b, (((ca,), (cb,)), ((), ())), preferred_element_type=F32)


def shape(dims, dtype):
    return jax.ShapeDtypeStruct(dims, dtype)


VMEM = pl.BlockSpec(memory_space=pltpu.VMEM)
SMEM = pl.BlockSpec(memory_space=pltpu.SMEM)
ANY = pl.BlockSpec(memory_space=pl.ANY)


TINY = pl.CostEstimate(flops=1, transcendentals=0, bytes_accessed=1)


LONG = pl.CostEstimate(flops=1 << 34, transcendentals=0, bytes_accessed=1 << 26)


def run(body, outs, *args, grid=(), specs=None, out_specs=None, scratch=(), name=None, cost=TINY, limit=56):
    return pl.pallas_call(
        body,
        out_shape=outs,
        grid=grid,
        in_specs=specs or [VMEM] * len(args),
        out_specs=out_specs or jax.tree.map(lambda _: VMEM, outs),
        scratch_shapes=list(scratch),
        name=name,
        cost_estimate=cost,
        compiler_params=pltpu.CompilerParams(vmem_limit_bytes=limit << 20),
    )(*args)


def pack_rows(ref, value):
    ref[...] = value.astype(BF16).reshape(ref.shape)


def in_vmem(value):
    return pltpu.with_memory_space_constraint(value, pltpu.VMEM)


def x_body(routes_ref, labels_ref, tokens_ref, table_ref, send_ref):
    ids = lax.broadcasted_iota(I32, (EXPERTS, TOK), 0)
    routes = (routes_ref[0:1, :], routes_ref[1:2, :])
    hit = [r == ids for r in routes]
    hits = jnp.where(hit[0], 1.0, jnp.where(hit[1], 1.0, 0.0)).astype(BF16)
    t_row = lax.broadcasted_iota(I32, (TOK, TOK), 0)
    t_col = lax.broadcasted_iota(I32, (TOK, TOK), 1)
    before = jnp.where(t_row < t_col, 1.0, 0.0).astype(BF16)
    earlier = dot(hits, before, 1, 0)
    slot = lax.broadcasted_iota(I32, (HALF, TOK), 0)
    both = jnp.zeros((HALF, TOK), F32)
    for k in range(2):
        pos = jnp.sum(jnp.where(hit[k], earlier, 0.0), axis=0, keepdims=True)
        row = routes[k] * (2 * CAP) + pos.astype(I32)
        table = jnp.where(slot == row, 1.0, jnp.where(slot == row + CAP, 1.0, 0.0))
        table_ref[k] = table.astype(BF16)
        both = both + table
    rows = dot(both.astype(BF16), tokens_ref[...], 1, 0)
    labels = labels_ref[...]
    high = lax.shift_right_logical(labels, 8)
    low = labels - high * 256
    digits = jnp.concatenate(
        [high.astype(F32), low.astype(F32), jnp.zeros((4, 120), F32)], axis=1
    ).astype(BF16)
    place = lax.broadcasted_iota(I32, (HALF, 4), 0)
    image = lax.broadcasted_iota(I32, (HALF, 4), 1)
    chip = lax.shift_right_logical(place * 6554, 16)
    spread = jnp.where(place - CAP * chip == image, 1.0, 0.0).astype(BF16)
    pack_rows(send_ref, jnp.concatenate([rows, dot(spread, digits, 1, 0)], axis=1))


def g_body(table_ref, grad_ref, combine_ref, send_ref):
    table0, table1 = table_ref[0].astype(F32), table_ref[1].astype(F32)
    scale = jnp.sum(
        table0 * combine_ref[0:1, :] + table1 * combine_ref[1:2, :], axis=1, keepdims=True
    )
    pack_rows(send_ref, scale * dot((table0 + table1).astype(BF16), grad_ref[...], 1, 0))


HALVES = (slice(0, HALF), slice(HALF, ROWS))


def chunks(part, size):
    return [slice(n, n + size) for n in range(part.start, part.stop, size)]


def start_all(pairs, sems):
    copies = [pltpu.make_async_copy(s, d, sems.at[n]) for n, (s, d) in enumerate(pairs)]
    for copy in copies:
        copy.start()
    return copies


def forward_body(
    own_x, other_x, w1_in, w2_in, xs_out, hidden_out, slope_out, own_out, other_out,
    w1, w2, xs, hidden, slope, own, other, in_sems, out_sems,
):
    copies = start_all(((w1_in, w1), (w2_in, w2)), in_sems)
    saved = []
    for n, half in enumerate(HALVES):
        xs[half] = (own_x, other_x)[n][:, :, :D].reshape(HALF, D)
        if n == 0:
            copies[0].wait()

        def activate(i, carry):
            for low in (0, 160):
                rows = pl.ds(pl.multiple_of(half.start + low + i * 320, 160), 160)
                h = dot(xs[rows, :], w1[...], 1, 0)
                square = h * h
                bend = jnp.tanh(h * (ROOT_2_PI + (ROOT_2_PI * CUBIC) * square))
                act = 0.5 + 0.5 * bend
                hidden[rows, :] = (h * act).astype(BF16)
                tilt = (1.0 - bend * bend) * (
                    0.5 * ROOT_2_PI + (1.5 * ROOT_2_PI * CUBIC) * square
                )
                slope[rows, :] = (act + h * tilt).astype(BF16)
            return carry

        lax.fori_loop(0, 2, activate, 0)
        saved += start_all(
            [(v.at[half], o.at[half]) for v, o in ((xs, xs_out), (hidden, hidden_out), (slope, slope_out))],
            out_sems.at[n],
        )
        if n == 0:
            copies[1].wait()
        for rows in chunks(half, 160):
            part = dot(hidden[rows, :], w2[...], 1, 0)
            there = slice(rows.start - half.start, rows.stop - half.start)
            if n == 0:
                own[there, :] = part
            else:
                other[there, :] = part.astype(BF16)
        saved += start_all([((own, other)[n], (own_out, other_out)[n])], out_sems.at[2 + n])
    for copy in saved:
        copy.wait()


def backward_body(
    own_g, other_g, slope_in, w1_in, w2_in, hidden_in, xs_in, own_out, other_out, dw2_out, dw1_out,
    slope, w1, w2, hidden, xs, gs, d_pre, own, other, dw2, dw1, in_sems, out_sems,
):
    first, last = HALVES
    pairs = (
        (w2_in, w2), (slope_in.at[first], slope.at[first]), (w1_in, w1),
        (slope_in.at[last], slope.at[last]), (hidden_in, hidden), (xs_in, xs),
    )
    copies = start_all(pairs, in_sems)
    saved = []
    for n, half in enumerate(HALVES):
        gs[half] = (own_g, other_g)[n][...].reshape(HALF, D)
        if n == 0:
            copies[0].wait()
        copies[(1, 3)[n]].wait()
        for rows in chunks(half, 320):
            d_h = dot(gs[rows, :], w2[...], 1, 1)
            d_pre[rows, :] = (d_h * slope[rows, :].astype(F32)).astype(BF16)
        if n == 0:
            copies[2].wait()
        for rows in chunks(half, 320):
            part = dot(d_pre[rows, :], w1[...], 1, 1)
            there = slice(rows.start - half.start, rows.stop - half.start)
            if n == 0:
                own[there, :] = part
            else:
                other[there, :] = part.astype(BF16)
        saved += start_all([((own, other)[n], (own_out, other_out)[n])], out_sems.at[n])
    grads = ((hidden, gs, dw2, dw2_out), (xs, d_pre, dw1, dw1_out))
    for n, (left, right, grad, grad_out) in enumerate(grads):
        copies[4 + n].wait()
        for m, cols in enumerate(HALVES):
            grad[cols, :] = dot(left[:, cols], right[...], 0, 0).astype(BF16)
            saved += start_all([(grad.at[cols], grad_out.at[cols])], out_sems.at[2 + 2 * n + m])
    for copy in saved:
        copy.wait()


SQUARE = (ROWS, D)
SENT = (shape((HALF, D), F32), shape((HALF, D), BF16))


def expert_kernel(body, own, other, rest, outs, name):
    inner = 2 if name == "backward" else 0
    scratch = [pltpu.VMEM(SQUARE, BF16)] * (len(rest) + inner)
    scratch += [pltpu.VMEM(out.shape, out.dtype) for out in outs]
    scratch += [pltpu.SemaphoreType.DMA((6,)), pltpu.SemaphoreType.DMA((6, 3))]
    return run(
        body,
        outs,
        in_vmem(own),
        in_vmem(other),
        *rest,
        specs=[VMEM] * 2 + [ANY] * len(rest),
        out_specs=tuple([ANY] * len(outs)),
        scratch=scratch,
        name=name,
    )


def mark_body(in_ref, out_ref):
    out_ref[0] = in_ref[0]


def add_body(own_ref, other_ref, send_ref):
    rows = pl.ds(pl.multiple_of(pl.program_id(0) * ADD_ROWS, ADD_ROWS), ADD_ROWS)
    pack_rows(send_ref, own_ref[...] + other_ref[rows, :].astype(F32))


ADD_ROWS = 320


def add_cores(own, other, name, cost=TINY):
    rows = pl.BlockSpec((ADD_ROWS, D), lambda i: (i, 0))
    return run(
        add_body,
        shape(PACKED, BF16),
        own,
        in_vmem(other),
        grid=(HALF // ADD_ROWS,),
        specs=[rows, VMEM],
        out_specs=pl.BlockSpec((ADD_ROWS // 2, 2, D), lambda i: (i, 0, 0)),
        name=name,
        cost=cost,
    )


def across(row):
    return jnp.sum(jnp.where(eye(), row, 0.0), axis=1, keepdims=True)


def along(column):
    return jnp.sum(jnp.where(eye(), column, 0.0), axis=0, keepdims=True)


def eye():
    return lax.broadcasted_iota(I32, (TOK, TOK), 0) == lax.broadcasted_iota(I32, (TOK, TOK), 1)


def mixed_body(table_ref, in_ref, tokens_ref, grad_ref, combine_ref, mixed_ref, dc_ref, sum_ref):
    rows = in_ref[...].reshape(HALF, D)
    vals0 = dot(table_ref[0], rows, 0, 0)
    vals1 = dot(table_ref[1], rows, 0, 0)
    grad = grad_ref[...].astype(F32)
    dc_ref[0:1, :] = along(jnp.sum(grad * vals0, axis=1, keepdims=True))
    dc_ref[1:2, :] = along(jnp.sum(grad * vals1, axis=1, keepdims=True))
    mixed = (
        tokens_ref[...].astype(F32)
        + (across(combine_ref[0:1, :]) * vals0 + across(combine_ref[1:2, :]) * vals1)
    ).astype(BF16)
    mixed_ref[...] = mixed
    sum_ref[...] = jnp.sum(mixed.astype(F32), axis=0, keepdims=True)


def tokens_body(table_ref, in_ref, grad_ref, out_ref):
    rows = in_ref[...].reshape(HALF, D)
    table = (table_ref[0].astype(F32) + table_ref[1].astype(F32)).astype(BF16)
    out_ref[...] = (grad_ref[...].astype(F32) + dot(table, rows, 0, 0)).astype(BF16)


def in_order(here, parts, j):
    pick = parts[0]
    for shift in (1, 2, 3):
        pick = jnp.where((here + shift) % 4 == j, parts[shift], pick)
    return pick


def y_parts(mine):
    return [in_vmem(mine)] + [
        in_vmem(lax.ppermute(mine, Y, [((i + shift) % 4, i) for i in range(4)]))
        for shift in (1, 2, 3)
    ]


def centered(pooled):
    away = pooled - jnp.mean(pooled, axis=1, keepdims=True)
    return away, lax.rsqrt(jnp.mean(away * away, axis=1, keepdims=True) + EPS)


CLASS_CUTS = (0, 640, 1152, 1664, COLS)


def head_body(
    here_ref, p0, p1, p2, p3, target_ref, weight_ref, w_in, pooled_ref, part_ref, send_ref, w_ref, sems
):
    spans = [slice(low, high) for low, high in zip(CLASS_CUTS, CLASS_CUTS[1:])]
    copies = start_all([(w_in.at[:, span], w_ref.at[:, span]) for span in spans], sems)
    here = here_ref[0]
    parts = [p[...] for p in (p0, p1, p2, p3)]
    for j in range(4):
        pooled_ref[j : j + 1, :] = in_order(here, parts, j) * (1.0 / PATCHES)
    away, scale = centered(pooled_ref[...])
    normed = (away * scale).astype(BF16)
    zeros = jnp.zeros((4, 48), BF16)
    for d in range(16):
        send_ref[d, :, COLS : COLS + 128] = jnp.concatenate(
            [normed[:, 80 * d : 80 * d + 80], zeros], axis=1
        )
    loss = jnp.zeros((4, 1), F32)
    d_normed = jnp.zeros((4, D), F32)
    for span, copy in zip(spans, copies):
        copy.wait()
        logits = dot(normed, w_ref[:, span], 1, 0)
        hit = target_ref[:, span] > 0.5
        signed = jnp.where(hit, -logits, logits)
        small = jnp.exp(-jnp.abs(signed))
        nll = jnp.maximum(signed, 0.0) + jnp.log1p(small)
        inverse = 1.0 / (1.0 + small)
        miss = jnp.where(signed >= 0.0, 1.0, small) * inverse
        keep = jnp.where(signed >= 0.0, small, 1.0) * inverse
        weight = weight_ref[:, span]
        loss = loss + jnp.sum(weight * (miss * miss) * nll, axis=1, keepdims=True)
        slope = weight * (2.0 * miss * keep * nll + miss * miss) * miss
        d_logits = jnp.where(hit, -slope, slope).astype(BF16)
        d_normed = d_normed + dot(d_logits, w_ref[:, span], 1, 1)
        for d in range(16):
            send_ref[d, :, span] = d_logits
    part_ref[:, :D] = d_normed
    part_ref[:, D:] = jnp.broadcast_to(loss, (4, 128))


def pooled_body(here_ref, m0, m1, m2, m3, pooled_ref, d_ref, loss_ref):
    here = here_ref[0]
    parts = [m[...] for m in (m0, m1, m2, m3)]
    total = in_order(here, parts, 0)
    for j in (1, 2, 3):
        total = total + in_order(here, parts, j)
    away, scale = centered(pooled_ref[...])
    normed = away * scale
    d_normed = total[:, :D]
    mean = jnp.mean(d_normed, axis=1, keepdims=True)
    along = jnp.mean(d_normed * normed, axis=1, keepdims=True)
    d_ref[...] = scale * (d_normed - mean - normed * along)
    diagonal = lax.broadcasted_iota(I32, (4, 4), 0) == lax.broadcasted_iota(I32, (4, 4), 1)
    loss_ref[...] = jnp.sum(
        jnp.where(diagonal, total[:, D : D + 1], 0.0), axis=0, keepdims=True
    )


def effective_of(counts):
    return (1.0 - BETA) / (1.0 - jnp.exp((counts + 1.0) * LOG_BETA))


def label_body(first_ref, digits_ref, labels_ref, target_ref, weight_ref):
    ids = (lax.broadcasted_iota(I32, (1, COLS), 1) + first_ref[0]).astype(F32)
    own = labels_ref[...].astype(F32)
    target = own[:, 0:1] == ids
    for n in range(1, 4):
        target = target | (own[:, n : n + 1] == ids)
    target_ref[...] = jnp.where(target, 1.0, 0.0)
    digits = digits_ref[...].astype(F32)
    labels = digits[:, 0:4] * 256.0 + digits[:, 4:8]
    padded = jnp.concatenate([labels, jnp.zeros((IMAGES, 124), F32)], axis=1)
    turned = jnp.concatenate([padded, jnp.zeros((128 - IMAGES, 128), F32)], axis=0).T
    columns = [labels[:, n : n + 1] for n in range(4)]
    rows = [turned[n : n + 1, :IMAGES] for n in range(4)]

    def fresh_of(entries):
        out = [jnp.ones_like(entries[0])]
        for n in range(1, 4):
            keep = out[0]
            for m in range(n):
                keep = jnp.where(entries[m] == entries[n], 0.0, keep)
            out.append(keep)
        return out

    fresh, fresh_row = fresh_of(columns), fresh_of(rows)
    counts = jnp.zeros((IMAGES, COLS), F32)
    excess = jnp.zeros((IMAGES, 1), F32)
    base = effective_of(jnp.zeros((IMAGES, 1), F32))
    for n in range(4):
        counts = counts + jnp.where(columns[n] == ids, fresh[n], 0.0)
        same = jnp.zeros((IMAGES, IMAGES), F32)
        for m in range(4):
            same = same + jnp.where(columns[n] == rows[m], fresh_row[m], 0.0)
        count = jnp.sum(same, axis=1, keepdims=True)
        excess = excess + fresh[n] * (effective_of(count) - base) / count
    total = CLASSES * base[0:1, :] + jnp.sum(excess, axis=0, keepdims=True)
    weight_ref[...] = effective_of(jnp.sum(counts, axis=0, keepdims=True)) * (CLASSES / total)


def chip_swap(packed):
    dims = packed.shape
    blocks = packed.reshape(CHIPS, CAP // 2, 2, dims[-1])
    return lax.all_to_all(blocks, CHIP, 0, 0, tiled=True).reshape(dims)


def core_swap(rows):
    return lax.ppermute(rows, "core", SWAP)


def shards(tokens, routes, combine, w_in, w_out, out_grad, head_w, labels):
    here = lax.axis_index(Y).astype(I32).reshape(1)
    first_class = (lax.axis_index(EX) * COLS).astype(I32).reshape(1)
    combine = combine.T
    table, x_send = run(
        x_body,
        (shape((2, HALF, TOK), BF16), shape(PACKED_X, BF16)),
        routes.T,
        labels,
        tokens,
        name="dispatch_x",
    )
    x_in = chip_swap(x_send)
    g_send = run(g_body, shape(PACKED, BF16), table, out_grad, combine, name="dispatch_g")
    x_in, g_send = lax.optimization_barrier((x_in, g_send))
    g_in = chip_swap(g_send)
    square = shape(SQUARE, BF16)
    xs, hidden, slope, own, other = expert_kernel(
        forward_body, x_in, core_swap(x_in), (w_in, w_out), (square, square, square, *SENT), "forward"
    )
    other = core_swap(other)
    digits = x_in.reshape(16, 2 * CAP, 2, WIDE)[:, :2, :, D:].reshape(IMAGES, 128)
    targets, class_weight = run(
        label_body,
        (shape((4, COLS), F32), shape((1, COLS), F32)),
        first_class,
        digits,
        labels,
        specs=[SMEM, VMEM, VMEM],
        name="labels",
    )
    g_in, targets, class_weight, mark = lax.optimization_barrier(
        (g_in, targets, class_weight, here)
    )
    mark = run(mark_body, shape((1,), I32), mark, specs=[SMEM], out_specs=SMEM, name="mark", cost=LONG)
    own, mark = lax.optimization_barrier((own, mark))
    out_in = chip_swap(add_cores(own, other, "add_out"))
    own, other, d_w_out, d_w_in = expert_kernel(
        backward_body,
        g_in,
        core_swap(g_in),
        (slope, w_in, w_out, hidden, xs),
        (*SENT, square, square),
        "backward",
    )
    other = core_swap(other)
    mixed_out, d_combine, token_sum = run(
        mixed_body,
        (shape((TOK, D), BF16), shape((2, TOK), F32), shape((1, D), F32)),
        table,
        in_vmem(out_in),
        tokens,
        out_grad,
        combine,
        name="mixed",
        cost=LONG,
    )
    token_sum = lax.psum(token_sum, "core")
    own, token_sum = lax.optimization_barrier((own, token_sum))
    rows_send = add_cores(own, other, "add_rows")
    rows_send, *sums = lax.optimization_barrier((rows_send, *y_parts(token_sum)))
    rows_in = chip_swap(rows_send)
    pooled, part, dp_send = run(
        head_body,
        (shape((4, D), F32), shape((4, D + 128), F32), shape((16, 4, COLS + 128), BF16)),
        here,
        *sums,
        targets,
        class_weight,
        head_w,
        specs=[SMEM] + [VMEM] * 6 + [ANY],
        scratch=[pltpu.VMEM((D, COLS), BF16), pltpu.SemaphoreType.DMA((4,))],
        name="head",
    )
    messages = y_parts(lax.psum(part, "core"))
    d_pooled, losses = run(
        pooled_body,
        (shape((4, D), F32), shape((1, 4), F32)),
        here,
        *messages,
        pooled,
        specs=[SMEM] + [VMEM] * 5,
        name="d_pooled",
    )
    dp_send, rows_in, d_pooled = lax.optimization_barrier((dp_send, rows_in, d_pooled))
    dp_in = lax.all_to_all(dp_send, "dp", 0, 0, tiled=True).reshape(IMAGES, COLS + 128)
    d_tokens = run(tokens_body, shape((TOK, D), BF16), table, in_vmem(rows_in), out_grad, name="d_tokens")
    d_head = dot(dp_in[:, COLS : COLS + 80], dp_in[:, :COLS], 0, 0).astype(BF16)
    return (mixed_out, d_tokens, d_combine.T, d_w_in, d_w_out, losses.reshape(4), d_pooled, d_head)


def solution(mesh):
    grid = Mesh(mesh.devices.reshape(16, 2, 2, 2), ALL)
    rows = P(ALL, None)
    in_specs = (rows, rows, rows, P(None, ALL), rows, rows, P(None, EX), P("dp", None))
    out_specs = (
        rows,
        rows,
        rows,
        P(None, ALL),
        rows,
        P("dp"),
        P("dp", None),
        P("dp", EX),
    )
    return jax.shard_map(shards, mesh=grid, in_specs=in_specs, out_specs=out_specs, check_vma=False)
```

```python
import math

import jax
import jax.numpy as jnp
from jax import lax
from jax.experimental import pallas as pl
from jax.experimental.pallas import tpu as pltpu
from jax.sharding import Mesh, PartitionSpec as P

D = 1280
EXPERTS = 32
PATCHES = 256
CLASSES = 17408
CAP = 10
CHIPS = 64
IMAGES = 64
TOK = 128
HALF = CHIPS * CAP
ROWS = 2 * HALF
COLS = CLASSES // 8
BETA = 0.99
LOG_BETA = math.log(BETA)
EPS = 1e-06

CHIP = ("dp", "yh", "yl")
Y = ("yh", "yl")
EX = ("yh", "yl", "core")
ALL = ("dp", "yh", "yl", "core")
SWAP = [(0, 1), (1, 0)]
F32 = jnp.float32
BF16 = jnp.bfloat16
I32 = jnp.int32
PACKED = (HALF // 2, 2, D)
WIDE = D + 128
PACKED_X = (HALF // 2, 2, WIDE)
ROOT_2_PI = 0.7978845608028654
CUBIC = 0.044715


def dot(a, b, ca, cb):
    return lax.dot_general(a, b, (((ca,), (cb,)), ((), ())), preferred_element_type=F32)


def shape(dims, dtype):
    return jax.ShapeDtypeStruct(dims, dtype)


VMEM = pl.BlockSpec(memory_space=pltpu.VMEM)
SMEM = pl.BlockSpec(memory_space=pltpu.SMEM)
ANY = pl.BlockSpec(memory_space=pl.ANY)


TINY = pl.CostEstimate(flops=1, transcendentals=0, bytes_accessed=1)


LONG = pl.CostEstimate(flops=1 << 34, transcendentals=0, bytes_accessed=1 << 26)


def run(body, outs, *args, grid=(), specs=None, out_specs=None, scratch=(), name=None, cost=TINY, limit=56):
    return pl.pallas_call(
        body,
        out_shape=outs,
        grid=grid,
        in_specs=specs or [VMEM] * len(args),
        out_specs=out_specs or jax.tree.map(lambda _: VMEM, outs),
        scratch_shapes=list(scratch),
        name=name,
        cost_estimate=cost,
        compiler_params=pltpu.CompilerParams(vmem_limit_bytes=limit << 20),
    )(*args)


def pack_rows(ref, value):
    ref[...] = value.astype(BF16).reshape(ref.shape)


def in_vmem(value):
    return pltpu.with_memory_space_constraint(value, pltpu.VMEM)


def x_body(routes_ref, labels_ref, tokens_ref, table_ref, send_ref):
    ids = lax.broadcasted_iota(I32, (EXPERTS, TOK), 0)
    routes = (routes_ref[0:1, :], routes_ref[1:2, :])
    hit = [r == ids for r in routes]
    hits = jnp.where(hit[0], 1.0, jnp.where(hit[1], 1.0, 0.0)).astype(BF16)
    t_row = lax.broadcasted_iota(I32, (TOK, TOK), 0)
    t_col = lax.broadcasted_iota(I32, (TOK, TOK), 1)
    before = jnp.where(t_row < t_col, 1.0, 0.0).astype(BF16)
    earlier = dot(hits, before, 1, 0)
    slot = lax.broadcasted_iota(I32, (HALF, TOK), 0)
    both = jnp.zeros((HALF, TOK), F32)
    for k in range(2):
        pos = jnp.sum(jnp.where(hit[k], earlier, 0.0), axis=0, keepdims=True)
        row = routes[k] * (2 * CAP) + pos.astype(I32)
        table = jnp.where(slot == row, 1.0, jnp.where(slot == row + CAP, 1.0, 0.0))
        table_ref[k] = table.astype(BF16)
        both = both + table
    rows = dot(both.astype(BF16), tokens_ref[...], 1, 0)
    labels = labels_ref[...]
    high = lax.shift_right_logical(labels, 8)
    low = labels - high * 256
    digits = jnp.concatenate(
        [high.astype(F32), low.astype(F32), jnp.zeros((4, 120), F32)], axis=1
    ).astype(BF16)
    place = lax.broadcasted_iota(I32, (HALF, 4), 0)
    image = lax.broadcasted_iota(I32, (HALF, 4), 1)
    chip = lax.shift_right_logical(place * 6554, 16)
    spread = jnp.where(place - CAP * chip == image, 1.0, 0.0).astype(BF16)
    pack_rows(send_ref, jnp.concatenate([rows, dot(spread, digits, 1, 0)], axis=1))


def g_body(table_ref, grad_ref, combine_ref, send_ref):
    table0, table1 = table_ref[0].astype(F32), table_ref[1].astype(F32)
    scale = jnp.sum(
        table0 * combine_ref[0:1, :] + table1 * combine_ref[1:2, :], axis=1, keepdims=True
    )
    pack_rows(send_ref, scale * dot((table0 + table1).astype(BF16), grad_ref[...], 1, 0))


HALVES = (slice(0, HALF), slice(HALF, ROWS))


def chunks(part, size):
    return [slice(n, n + size) for n in range(part.start, part.stop, size)]


def start_all(pairs, sems):
    copies = [pltpu.make_async_copy(s, d, sems.at[n]) for n, (s, d) in enumerate(pairs)]
    for copy in copies:
        copy.start()
    return copies


def forward_body(
    own_x, other_x, w1_in, w2_in, xs_out, hidden_out, slope_out, own_out, other_out,
    w1, w2, xs, hidden, slope, own, other, in_sems, out_sems,
):
    copies = start_all(((w1_in, w1), (w2_in, w2)), in_sems)
    saved = []
    for n, half in enumerate(HALVES):
        xs[half] = (own_x, other_x)[n][:, :, :D].reshape(HALF, D)
        if n == 0:
            copies[0].wait()

        def activate(i, carry):
            for low in (0, 160):
                rows = pl.ds(pl.multiple_of(half.start + low + i * 320, 160), 160)
                h = dot(xs[rows, :], w1[...], 1, 0)
                square = h * h
                bend = jnp.tanh(h * (ROOT_2_PI + (ROOT_2_PI * CUBIC) * square))
                act = 0.5 + 0.5 * bend
                hidden[rows, :] = (h * act).astype(BF16)
                tilt = (1.0 - bend * bend) * (
                    0.5 * ROOT_2_PI + (1.5 * ROOT_2_PI * CUBIC) * square
                )
                slope[rows, :] = (act + h * tilt).astype(BF16)
            return carry

        lax.fori_loop(0, 2, activate, 0)
        saved += start_all(
            [(v.at[half], o.at[half]) for v, o in ((xs, xs_out), (hidden, hidden_out), (slope, slope_out))],
            out_sems.at[n],
        )
        if n == 0:
            copies[1].wait()
        for rows in chunks(half, 160):
            part = dot(hidden[rows, :], w2[...], 1, 0)
            there = slice(rows.start - half.start, rows.stop - half.start)
            if n == 0:
                own[there, :] = part
            else:
                other[there, :] = part.astype(BF16)
        saved += start_all([((own, other)[n], (own_out, other_out)[n])], out_sems.at[2 + n])
    for copy in saved:
        copy.wait()


def backward_body(
    own_g, other_g, slope_in, w1_in, w2_in, hidden_in, xs_in, own_out, other_out, dw2_out, dw1_out,
    slope, w1, w2, hidden, xs, gs, d_pre, own, other, dw2, dw1, in_sems, out_sems,
):
    first, last = HALVES
    pairs = (
        (w2_in, w2), (slope_in.at[first], slope.at[first]), (w1_in, w1),
        (slope_in.at[last], slope.at[last]), (hidden_in, hidden), (xs_in, xs),
    )
    copies = start_all(pairs, in_sems)
    saved = []
    for n, half in enumerate(HALVES):
        gs[half] = (own_g, other_g)[n][...].reshape(HALF, D)
        if n == 0:
            copies[0].wait()
        copies[(1, 3)[n]].wait()
        for rows in chunks(half, 320):
            d_h = dot(gs[rows, :], w2[...], 1, 1)
            d_pre[rows, :] = (d_h * slope[rows, :].astype(F32)).astype(BF16)
        if n == 0:
            copies[2].wait()
        for rows in chunks(half, 320):
            part = dot(d_pre[rows, :], w1[...], 1, 1)
            there = slice(rows.start - half.start, rows.stop - half.start)
            if n == 0:
                own[there, :] = part
            else:
                other[there, :] = part.astype(BF16)
        saved += start_all([((own, other)[n], (own_out, other_out)[n])], out_sems.at[n])
    grads = ((hidden, gs, dw2, dw2_out), (xs, d_pre, dw1, dw1_out))
    for n, (left, right, grad, grad_out) in enumerate(grads):
        copies[4 + n].wait()
        for m, cols in enumerate(HALVES):
            grad[cols, :] = dot(left[:, cols], right[...], 0, 0).astype(BF16)
            saved += start_all([(grad.at[cols], grad_out.at[cols])], out_sems.at[2 + 2 * n + m])
    for copy in saved:
        copy.wait()


SQUARE = (ROWS, D)
SENT = (shape((HALF, D), F32), shape((HALF, D), BF16))


def expert_kernel(body, own, other, rest, outs, name):
    inner = 2 if name == "backward" else 0
    scratch = [pltpu.VMEM(SQUARE, BF16)] * (len(rest) + inner)
    scratch += [pltpu.VMEM(out.shape, out.dtype) for out in outs]
    scratch += [pltpu.SemaphoreType.DMA((6,)), pltpu.SemaphoreType.DMA((6, 3))]
    return run(
        body,
        outs,
        in_vmem(own),
        in_vmem(other),
        *rest,
        specs=[VMEM] * 2 + [ANY] * len(rest),
        out_specs=tuple([ANY] * len(outs)),
        scratch=scratch,
        name=name,
    )


def mark_body(in_ref, out_ref):
    out_ref[0] = in_ref[0]


def add_body(own_ref, other_ref, send_ref):
    rows = pl.ds(pl.multiple_of(pl.program_id(0) * ADD_ROWS, ADD_ROWS), ADD_ROWS)
    pack_rows(send_ref, own_ref[...] + other_ref[rows, :].astype(F32))


ADD_ROWS = 320


def add_cores(own, other, name, cost=TINY):
    rows = pl.BlockSpec((ADD_ROWS, D), lambda i: (i, 0))
    return run(
        add_body,
        shape(PACKED, BF16),
        own,
        in_vmem(other),
        grid=(HALF // ADD_ROWS,),
        specs=[rows, VMEM],
        out_specs=pl.BlockSpec((ADD_ROWS // 2, 2, D), lambda i: (i, 0, 0)),
        name=name,
        cost=cost,
    )


def across(row):
    return jnp.sum(jnp.where(eye(), row, 0.0), axis=1, keepdims=True)


def along(column):
    return jnp.sum(jnp.where(eye(), column, 0.0), axis=0, keepdims=True)


def eye():
    return lax.broadcasted_iota(I32, (TOK, TOK), 0) == lax.broadcasted_iota(I32, (TOK, TOK), 1)


def mixed_body(table_ref, in_ref, tokens_ref, grad_ref, combine_ref, mixed_ref, dc_ref, sum_ref):
    rows = in_ref[...].reshape(HALF, D)
    vals0 = dot(table_ref[0], rows, 0, 0)
    vals1 = dot(table_ref[1], rows, 0, 0)
    grad = grad_ref[...].astype(F32)
    dc_ref[0:1, :] = along(jnp.sum(grad * vals0, axis=1, keepdims=True))
    dc_ref[1:2, :] = along(jnp.sum(grad * vals1, axis=1, keepdims=True))
    mixed = (
        tokens_ref[...].astype(F32)
        + (across(combine_ref[0:1, :]) * vals0 + across(combine_ref[1:2, :]) * vals1)
    ).astype(BF16)
    mixed_ref[...] = mixed
    sum_ref[...] = jnp.sum(mixed.astype(F32), axis=0, keepdims=True)


def tokens_body(table_ref, in_ref, grad_ref, out_ref):
    rows = in_ref[...].reshape(HALF, D)
    table = (table_ref[0].astype(F32) + table_ref[1].astype(F32)).astype(BF16)
    out_ref[...] = (grad_ref[...].astype(F32) + dot(table, rows, 0, 0)).astype(BF16)


def in_order(here, parts, j):
    pick = parts[0]
    for shift in (1, 2, 3):
        pick = jnp.where((here + shift) % 4 == j, parts[shift], pick)
    return pick


def y_parts(mine):
    return [in_vmem(mine)] + [
        in_vmem(lax.ppermute(mine, Y, [((i + shift) % 4, i) for i in range(4)]))
        for shift in (1, 2, 3)
    ]


def centered(pooled):
    away = pooled - jnp.mean(pooled, axis=1, keepdims=True)
    return away, lax.rsqrt(jnp.mean(away * away, axis=1, keepdims=True) + EPS)


CLASS_CUTS = (0, 640, 1152, 1664, COLS)


def head_body(
    here_ref, p0, p1, p2, p3, target_ref, weight_ref, w_in, pooled_ref, part_ref, send_ref, w_ref, sems
):
    spans = [slice(low, high) for low, high in zip(CLASS_CUTS, CLASS_CUTS[1:])]
    copies = start_all([(w_in.at[:, span], w_ref.at[:, span]) for span in spans], sems)
    here = here_ref[0]
    parts = [p[...] for p in (p0, p1, p2, p3)]
    for j in range(4):
        pooled_ref[j : j + 1, :] = in_order(here, parts, j) * (1.0 / PATCHES)
    away, scale = centered(pooled_ref[...])
    normed = (away * scale).astype(BF16)
    zeros = jnp.zeros((4, 48), BF16)
    for d in range(16):
        send_ref[d, :, COLS : COLS + 128] = jnp.concatenate(
            [normed[:, 80 * d : 80 * d + 80], zeros], axis=1
        )
    loss = jnp.zeros((4, 1), F32)
    d_normed = jnp.zeros((4, D), F32)
    for span, copy in zip(spans, copies):
        copy.wait()
        logits = dot(normed, w_ref[:, span], 1, 0)
        hit = target_ref[:, span] > 0.5
        signed = jnp.where(hit, -logits, logits)
        small = jnp.exp(-jnp.abs(signed))
        nll = jnp.maximum(signed, 0.0) + jnp.log1p(small)
        inverse = 1.0 / (1.0 + small)
        miss = jnp.where(signed >= 0.0, 1.0, small) * inverse
        keep = jnp.where(signed >= 0.0, small, 1.0) * inverse
        weight = weight_ref[:, span]
        loss = loss + jnp.sum(weight * (miss * miss) * nll, axis=1, keepdims=True)
        slope = weight * (2.0 * miss * keep * nll + miss * miss) * miss
        d_logits = jnp.where(hit, -slope, slope).astype(BF16)
        d_normed = d_normed + dot(d_logits, w_ref[:, span], 1, 1)
        for d in range(16):
            send_ref[d, :, span] = d_logits
    part_ref[:, :D] = d_normed
    part_ref[:, D:] = jnp.broadcast_to(loss, (4, 128))


def pooled_body(here_ref, m0, m1, m2, m3, pooled_ref, d_ref, loss_ref):
    here = here_ref[0]
    parts = [m[...] for m in (m0, m1, m2, m3)]
    total = in_order(here, parts, 0)
    for j in (1, 2, 3):
        total = total + in_order(here, parts, j)
    away, scale = centered(pooled_ref[...])
    normed = away * scale
    d_normed = total[:, :D]
    mean = jnp.mean(d_normed, axis=1, keepdims=True)
    along = jnp.mean(d_normed * normed, axis=1, keepdims=True)
    d_ref[...] = scale * (d_normed - mean - normed * along)
    diagonal = lax.broadcasted_iota(I32, (4, 4), 0) == lax.broadcasted_iota(I32, (4, 4), 1)
    loss_ref[...] = jnp.sum(
        jnp.where(diagonal, total[:, D : D + 1], 0.0), axis=0, keepdims=True
    )


def effective_of(counts):
    return (1.0 - BETA) / (1.0 - jnp.exp((counts + 1.0) * LOG_BETA))


def label_body(first_ref, digits_ref, labels_ref, target_ref, weight_ref):
    ids = (lax.broadcasted_iota(I32, (1, COLS), 1) + first_ref[0]).astype(F32)
    own = labels_ref[...].astype(F32)
    target = own[:, 0:1] == ids
    for n in range(1, 4):
        target = target | (own[:, n : n + 1] == ids)
    target_ref[...] = jnp.where(target, 1.0, 0.0)
    digits = digits_ref[...].astype(F32)
    labels = digits[:, 0:4] * 256.0 + digits[:, 4:8]
    padded = jnp.concatenate([labels, jnp.zeros((IMAGES, 124), F32)], axis=1)
    turned = jnp.concatenate([padded, jnp.zeros((128 - IMAGES, 128), F32)], axis=0).T
    columns = [labels[:, n : n + 1] for n in range(4)]
    rows = [turned[n : n + 1, :IMAGES] for n in range(4)]

    def fresh_of(entries):
        out = [jnp.ones_like(entries[0])]
        for n in range(1, 4):
            keep = out[0]
            for m in range(n):
                keep = jnp.where(entries[m] == entries[n], 0.0, keep)
            out.append(keep)
        return out

    fresh, fresh_row = fresh_of(columns), fresh_of(rows)
    counts = jnp.zeros((IMAGES, COLS), F32)
    excess = jnp.zeros((IMAGES, 1), F32)
    base = effective_of(jnp.zeros((IMAGES, 1), F32))
    for n in range(4):
        counts = counts + jnp.where(columns[n] == ids, fresh[n], 0.0)
        same = jnp.zeros((IMAGES, IMAGES), F32)
        for m in range(4):
            same = same + jnp.where(columns[n] == rows[m], fresh_row[m], 0.0)
        count = jnp.sum(same, axis=1, keepdims=True)
        excess = excess + fresh[n] * (effective_of(count) - base) / count
    total = CLASSES * base[0:1, :] + jnp.sum(excess, axis=0, keepdims=True)
    weight_ref[...] = effective_of(jnp.sum(counts, axis=0, keepdims=True)) * (CLASSES / total)


def chip_swap(packed):
    dims = packed.shape
    blocks = packed.reshape(CHIPS, CAP // 2, 2, dims[-1])
    return lax.all_to_all(blocks, CHIP, 0, 0, tiled=True).reshape(dims)


def core_swap(rows):
    return lax.ppermute(rows, "core", SWAP)


def shards(tokens, routes, combine, w_in, w_out, out_grad, head_w, labels):
    here = lax.axis_index(Y).astype(I32).reshape(1)
    first_class = (lax.axis_index(EX) * COLS).astype(I32).reshape(1)
    combine = combine.T
    table, x_send = run(
        x_body,
        (shape((2, HALF, TOK), BF16), shape(PACKED_X, BF16)),
        routes.T,
        labels,
        tokens,
        name="dispatch_x",
    )
    x_in = chip_swap(x_send)
    g_send = run(g_body, shape(PACKED, BF16), table, out_grad, combine, name="dispatch_g")
    x_in, g_send = lax.optimization_barrier((x_in, g_send))
    g_in = chip_swap(g_send)
    square = shape(SQUARE, BF16)
    xs, hidden, slope, own, other = expert_kernel(
        forward_body, x_in, core_swap(x_in), (w_in, w_out), (square, square, square, *SENT), "forward"
    )
    other = core_swap(other)
    digits = x_in.reshape(16, 2 * CAP, 2, WIDE)[:, :2, :, D:].reshape(IMAGES, 128)
    targets, class_weight = run(
        label_body,
        (shape((4, COLS), F32), shape((1, COLS), F32)),
        first_class,
        digits,
        labels,
        specs=[SMEM, VMEM, VMEM],
        name="labels",
    )
    g_in, targets, class_weight, mark = lax.optimization_barrier(
        (g_in, targets, class_weight, here)
    )
    mark = run(mark_body, shape((1,), I32), mark, specs=[SMEM], out_specs=SMEM, name="mark", cost=LONG)
    own, mark = lax.optimization_barrier((own, mark))
    out_in = chip_swap(add_cores(own, other, "add_out"))
    own, other, d_w_out, d_w_in = expert_kernel(
        backward_body,
        g_in,
        core_swap(g_in),
        (slope, w_in, w_out, hidden, xs),
        (*SENT, square, square),
        "backward",
    )
    other = core_swap(other)
    mixed_out, d_combine, token_sum = run(
        mixed_body,
        (shape((TOK, D), BF16), shape((2, TOK), F32), shape((1, D), F32)),
        table,
        in_vmem(out_in),
        tokens,
        out_grad,
        combine,
        name="mixed",
        cost=LONG,
    )
    own, token_sum = lax.optimization_barrier((own, token_sum))
    rows_in = chip_swap(add_cores(own, other, "add_rows"))
    sums = y_parts(lax.psum(token_sum, "core"))
    pooled, part, dp_send = run(
        head_body,
        (shape((4, D), F32), shape((4, D + 128), F32), shape((16, 4, COLS + 128), BF16)),
        here,
        *sums,
        targets,
        class_weight,
        head_w,
        specs=[SMEM] + [VMEM] * 6 + [ANY],
        scratch=[pltpu.VMEM((D, COLS), BF16), pltpu.SemaphoreType.DMA((4,))],
        name="head",
    )
    part, rows_in = lax.optimization_barrier((lax.psum(part, "core"), rows_in))
    messages = y_parts(part)
    d_pooled, losses = run(
        pooled_body,
        (shape((4, D), F32), shape((1, 4), F32)),
        here,
        *messages,
        pooled,
        specs=[SMEM] + [VMEM] * 5,
        name="d_pooled",
    )
    dp_send, rows_in = lax.optimization_barrier((dp_send, rows_in))
    dp_in = lax.all_to_all(dp_send, "dp", 0, 0, tiled=True).reshape(IMAGES, COLS + 128)
    d_tokens = run(tokens_body, shape((TOK, D), BF16), table, in_vmem(rows_in), out_grad, name="d_tokens")
    d_head = dot(dp_in[:, COLS : COLS + 80], dp_in[:, :COLS], 0, 0).astype(BF16)
    return (mixed_out, d_tokens, d_combine.T, d_w_in, d_w_out, losses.reshape(4), d_pooled, d_head)


def solution(mesh):
    grid = Mesh(mesh.devices.reshape(16, 2, 2, 2), ALL)
    rows = P(ALL, None)
    in_specs = (rows, rows, rows, P(None, ALL), rows, rows, P(None, EX), P("dp", None))
    out_specs = (
        rows,
        rows,
        rows,
        P(None, ALL),
        rows,
        P("dp"),
        P("dp", None),
        P("dp", EX),
    )
    return jax.shard_map(shards, mesh=grid, in_specs=in_specs, out_specs=out_specs, check_vma=False)
```

```python
import math

import jax
import jax.numpy as jnp
from jax import lax
from jax.experimental import pallas as pl
from jax.experimental.pallas import tpu as pltpu
from jax.sharding import Mesh, PartitionSpec as P

D = 1280
EXPERTS = 32
PATCHES = 256
CLASSES = 17408
CAP = 10
CHIPS = 64
IMAGES = 64
TOK = 128
HALF = CHIPS * CAP
ROWS = 2 * HALF
COLS = CLASSES // 8
BETA = 0.99
LOG_BETA = math.log(BETA)
EPS = 1e-06

CHIP = ("dp", "yh", "yl")
Y = ("yh", "yl")
EX = ("yh", "yl", "core")
ALL = ("dp", "yh", "yl", "core")
SWAP = [(0, 1), (1, 0)]
F32 = jnp.float32
BF16 = jnp.bfloat16
I32 = jnp.int32
PACKED = (HALF // 2, 2, D)
WIDE = D + 128
PACKED_X = (HALF // 2, 2, WIDE)
ROOT_2_PI = 0.7978845608028654
CUBIC = 0.044715


def dot(a, b, ca, cb):
    return lax.dot_general(a, b, (((ca,), (cb,)), ((), ())), preferred_element_type=F32)


def shape(dims, dtype):
    return jax.ShapeDtypeStruct(dims, dtype)


VMEM = pl.BlockSpec(memory_space=pltpu.VMEM)
SMEM = pl.BlockSpec(memory_space=pltpu.SMEM)
ANY = pl.BlockSpec(memory_space=pl.ANY)


TINY = pl.CostEstimate(flops=1, transcendentals=0, bytes_accessed=1)


LONG = pl.CostEstimate(flops=1 << 34, transcendentals=0, bytes_accessed=1 << 26)


def run(body, outs, *args, grid=(), specs=None, out_specs=None, scratch=(), name=None, cost=TINY, limit=56):
    return pl.pallas_call(
        body,
        out_shape=outs,
        grid=grid,
        in_specs=specs or [VMEM] * len(args),
        out_specs=out_specs or jax.tree.map(lambda _: VMEM, outs),
        scratch_shapes=list(scratch),
        name=name,
        cost_estimate=cost,
        compiler_params=pltpu.CompilerParams(vmem_limit_bytes=limit << 20),
    )(*args)


def pack_rows(ref, value):
    ref[...] = value.astype(BF16).reshape(ref.shape)


def in_vmem(value):
    return pltpu.with_memory_space_constraint(value, pltpu.VMEM)


def x_body(routes_ref, labels_ref, tokens_ref, table_ref, send_ref):
    ids = lax.broadcasted_iota(I32, (EXPERTS, TOK), 0)
    routes = (routes_ref[0:1, :], routes_ref[1:2, :])
    hit = [r == ids for r in routes]
    hits = jnp.where(hit[0], 1.0, jnp.where(hit[1], 1.0, 0.0)).astype(BF16)
    t_row = lax.broadcasted_iota(I32, (TOK, TOK), 0)
    t_col = lax.broadcasted_iota(I32, (TOK, TOK), 1)
    before = jnp.where(t_row < t_col, 1.0, 0.0).astype(BF16)
    earlier = dot(hits, before, 1, 0)
    slot = lax.broadcasted_iota(I32, (HALF, TOK), 0)
    both = jnp.zeros((HALF, TOK), F32)
    for k in range(2):
        pos = jnp.sum(jnp.where(hit[k], earlier, 0.0), axis=0, keepdims=True)
        row = routes[k] * (2 * CAP) + pos.astype(I32)
        table = jnp.where(slot == row, 1.0, jnp.where(slot == row + CAP, 1.0, 0.0))
        table_ref[k] = table.astype(BF16)
        both = both + table
    rows = dot(both.astype(BF16), tokens_ref[...], 1, 0)
    labels = labels_ref[...]
    high = lax.shift_right_logical(labels, 8)
    low = labels - high * 256
    digits = jnp.concatenate(
        [high.astype(F32), low.astype(F32), jnp.zeros((4, 120), F32)], axis=1
    ).astype(BF16)
    place = lax.broadcasted_iota(I32, (HALF, 4), 0)
    image = lax.broadcasted_iota(I32, (HALF, 4), 1)
    chip = lax.shift_right_logical(place * 6554, 16)
    spread = jnp.where(place - CAP * chip == image, 1.0, 0.0).astype(BF16)
    pack_rows(send_ref, jnp.concatenate([rows, dot(spread, digits, 1, 0)], axis=1))


def g_body(table_ref, grad_ref, combine_ref, send_ref):
    table0, table1 = table_ref[0].astype(F32), table_ref[1].astype(F32)
    scale = jnp.sum(
        table0 * combine_ref[0:1, :] + table1 * combine_ref[1:2, :], axis=1, keepdims=True
    )
    pack_rows(send_ref, scale * dot((table0 + table1).astype(BF16), grad_ref[...], 1, 0))


HALVES = (slice(0, HALF), slice(HALF, ROWS))


def chunks(part, size):
    return [slice(n, n + size) for n in range(part.start, part.stop, size)]


def start_all(pairs, sems):
    copies = [pltpu.make_async_copy(s, d, sems.at[n]) for n, (s, d) in enumerate(pairs)]
    for copy in copies:
        copy.start()
    return copies


def forward_body(
    own_x, other_x, w1_in, w2_in, xs_out, hidden_out, slope_out, own_out, other_out,
    w1, w2, xs, hidden, slope, own, other, in_sems, out_sems,
):
    copies = start_all(((w1_in, w1), (w2_in, w2)), in_sems)
    saved = []
    for n, half in enumerate(HALVES):
        xs[half] = (own_x, other_x)[n][:, :, :D].reshape(HALF, D)
        if n == 0:
            copies[0].wait()

        def activate(i, carry):
            for low in (0, 160):
                rows = pl.ds(pl.multiple_of(half.start + low + i * 320, 160), 160)
                h = dot(xs[rows, :], w1[...], 1, 0)
                square = h * h
                bend = jnp.tanh(h * (ROOT_2_PI + (ROOT_2_PI * CUBIC) * square))
                act = 0.5 + 0.5 * bend
                hidden[rows, :] = (h * act).astype(BF16)
                tilt = (1.0 - bend * bend) * (
                    0.5 * ROOT_2_PI + (1.5 * ROOT_2_PI * CUBIC) * square
                )
                slope[rows, :] = (act + h * tilt).astype(BF16)
            return carry

        lax.fori_loop(0, 2, activate, 0)
        saved += start_all(
            [(v.at[half], o.at[half]) for v, o in ((xs, xs_out), (hidden, hidden_out), (slope, slope_out))],
            out_sems.at[n],
        )
        if n == 0:
            copies[1].wait()
        for rows in chunks(half, 160):
            part = dot(hidden[rows, :], w2[...], 1, 0)
            there = slice(rows.start - half.start, rows.stop - half.start)
            if n == 0:
                own[there, :] = part.astype(BF16)
            else:
                other[there, :] = part.astype(BF16)
        saved += start_all([((own, other)[n], (own_out, other_out)[n])], out_sems.at[2 + n])
    for copy in saved:
        copy.wait()


def backward_body(
    own_g, other_g, slope_in, w1_in, w2_in, hidden_in, xs_in, own_out, other_out, dw2_out, dw1_out,
    slope, w1, w2, hidden, xs, gs, d_pre, own, other, dw2, dw1, in_sems, out_sems,
):
    first, last = HALVES
    pairs = (
        (w2_in, w2), (slope_in.at[first], slope.at[first]), (w1_in, w1),
        (slope_in.at[last], slope.at[last]), (hidden_in, hidden), (xs_in, xs),
    )
    copies = start_all(pairs, in_sems)
    saved = []
    for n, half in enumerate(HALVES):
        gs[half] = (own_g, other_g)[n][...].reshape(HALF, D)
        if n == 0:
            copies[0].wait()
        copies[(1, 3)[n]].wait()
        for rows in chunks(half, 320):
            d_h = dot(gs[rows, :], w2[...], 1, 1)
            d_pre[rows, :] = (d_h * slope[rows, :].astype(F32)).astype(BF16)
        if n == 0:
            copies[2].wait()
        for rows in chunks(half, 320):
            part = dot(d_pre[rows, :], w1[...], 1, 1)
            there = slice(rows.start - half.start, rows.stop - half.start)
            if n == 0:
                own[there, :] = part.astype(BF16)
            else:
                other[there, :] = part.astype(BF16)
        saved += start_all([((own, other)[n], (own_out, other_out)[n])], out_sems.at[n])
    grads = ((hidden, gs, dw2, dw2_out), (xs, d_pre, dw1, dw1_out))
    for n, (left, right, grad, grad_out) in enumerate(grads):
        copies[4 + n].wait()
        for m, cols in enumerate(HALVES):
            grad[cols, :] = dot(left[:, cols], right[...], 0, 0).astype(BF16)
            saved += start_all([(grad.at[cols], grad_out.at[cols])], out_sems.at[2 + 2 * n + m])
    for copy in saved:
        copy.wait()


SQUARE = (ROWS, D)
SENT = (shape((HALF, D), BF16), shape((HALF, D), BF16))


def expert_kernel(body, own, other, rest, outs, name):
    inner = 2 if name == "backward" else 0
    scratch = [pltpu.VMEM(SQUARE, BF16)] * (len(rest) + inner)
    scratch += [pltpu.VMEM(out.shape, out.dtype) for out in outs]
    scratch += [pltpu.SemaphoreType.DMA((6,)), pltpu.SemaphoreType.DMA((6, 3))]
    return run(
        body,
        outs,
        in_vmem(own),
        in_vmem(other),
        *rest,
        specs=[VMEM] * 2 + [ANY] * len(rest),
        out_specs=tuple([ANY] * len(outs)),
        scratch=scratch,
        name=name,
    )


def mark_body(in_ref, out_ref):
    out_ref[0] = in_ref[0]


def add_body(own_ref, other_ref, send_ref):
    rows = pl.ds(pl.multiple_of(pl.program_id(0) * ADD_ROWS, ADD_ROWS), ADD_ROWS)
    pack_rows(send_ref, own_ref[...].astype(F32) + other_ref[rows, :].astype(F32))


ADD_ROWS = 320


def add_cores(own, other, name, cost=TINY):
    rows = pl.BlockSpec((ADD_ROWS, D), lambda i: (i, 0))
    return run(
        add_body,
        shape(PACKED, BF16),
        own,
        in_vmem(other),
        grid=(HALF // ADD_ROWS,),
        specs=[rows, VMEM],
        out_specs=pl.BlockSpec((ADD_ROWS // 2, 2, D), lambda i: (i, 0, 0)),
        name=name,
        cost=cost,
    )


def across(row):
    return jnp.sum(jnp.where(eye(), row, 0.0), axis=1, keepdims=True)


def along(column):
    return jnp.sum(jnp.where(eye(), column, 0.0), axis=0, keepdims=True)


def eye():
    return lax.broadcasted_iota(I32, (TOK, TOK), 0) == lax.broadcasted_iota(I32, (TOK, TOK), 1)


def mixed_body(table_ref, in_ref, tokens_ref, grad_ref, combine_ref, mixed_ref, dc_ref, sum_ref):
    rows = in_ref[...].reshape(HALF, D)
    vals0 = dot(table_ref[0], rows, 0, 0)
    vals1 = dot(table_ref[1], rows, 0, 0)
    grad = grad_ref[...].astype(F32)
    dc_ref[0:1, :] = along(jnp.sum(grad * vals0, axis=1, keepdims=True))
    dc_ref[1:2, :] = along(jnp.sum(grad * vals1, axis=1, keepdims=True))
    mixed = (
        tokens_ref[...].astype(F32)
        + (across(combine_ref[0:1, :]) * vals0 + across(combine_ref[1:2, :]) * vals1)
    ).astype(BF16)
    mixed_ref[...] = mixed
    sum_ref[...] = jnp.sum(mixed.astype(F32), axis=0, keepdims=True)


def tokens_body(table_ref, in_ref, grad_ref, out_ref):
    rows = in_ref[...].reshape(HALF, D)
    table = (table_ref[0].astype(F32) + table_ref[1].astype(F32)).astype(BF16)
    out_ref[...] = (grad_ref[...].astype(F32) + dot(table, rows, 0, 0)).astype(BF16)


def in_order(here, parts, j):
    pick = parts[0]
    for shift in (1, 2, 3):
        pick = jnp.where((here + shift) % 4 == j, parts[shift], pick)
    return pick


def y_parts(mine):
    return [in_vmem(mine)] + [
        in_vmem(lax.ppermute(mine, Y, [((i + shift) % 4, i) for i in range(4)]))
        for shift in (1, 2, 3)
    ]


def centered(pooled):
    away = pooled - jnp.mean(pooled, axis=1, keepdims=True)
    return away, lax.rsqrt(jnp.mean(away * away, axis=1, keepdims=True) + EPS)


CLASS_CUTS = (0, 640, 1152, 1664, COLS)


def head_body(
    here_ref, p0, p1, p2, p3, target_ref, weight_ref, w_in, pooled_ref, part_ref, send_ref, w_ref, sems
):
    spans = [slice(low, high) for low, high in zip(CLASS_CUTS, CLASS_CUTS[1:])]
    copies = start_all([(w_in.at[:, span], w_ref.at[:, span]) for span in spans], sems)
    here = here_ref[0]
    parts = [p[...] for p in (p0, p1, p2, p3)]
    for j in range(4):
        pooled_ref[j : j + 1, :] = in_order(here, parts, j) * (1.0 / PATCHES)
    away, scale = centered(pooled_ref[...])
    normed = (away * scale).astype(BF16)
    zeros = jnp.zeros((4, 48), BF16)
    for d in range(16):
        send_ref[d, :, COLS : COLS + 128] = jnp.concatenate(
            [normed[:, 80 * d : 80 * d + 80], zeros], axis=1
        )
    loss = jnp.zeros((4, 1), F32)
    d_normed = jnp.zeros((4, D), F32)
    for span, copy in zip(spans, copies):
        copy.wait()
        logits = dot(normed, w_ref[:, span], 1, 0)
        hit = target_ref[:, span] > 0.5
        signed = jnp.where(hit, -logits, logits)
        small = jnp.exp(-jnp.abs(signed))
        nll = jnp.maximum(signed, 0.0) + jnp.log1p(small)
        inverse = 1.0 / (1.0 + small)
        miss = jnp.where(signed >= 0.0, 1.0, small) * inverse
        keep = jnp.where(signed >= 0.0, small, 1.0) * inverse
        weight = weight_ref[:, span]
        loss = loss + jnp.sum(weight * (miss * miss) * nll, axis=1, keepdims=True)
        slope = weight * (2.0 * miss * keep * nll + miss * miss) * miss
        d_logits = jnp.where(hit, -slope, slope).astype(BF16)
        d_normed = d_normed + dot(d_logits, w_ref[:, span], 1, 1)
        for d in range(16):
            send_ref[d, :, span] = d_logits
    part_ref[:, :D] = d_normed
    part_ref[:, D:] = jnp.broadcast_to(loss, (4, 128))


def pooled_body(here_ref, m0, m1, m2, m3, pooled_ref, d_ref, loss_ref):
    here = here_ref[0]
    parts = [m[...] for m in (m0, m1, m2, m3)]
    total = in_order(here, parts, 0)
    for j in (1, 2, 3):
        total = total + in_order(here, parts, j)
    away, scale = centered(pooled_ref[...])
    normed = away * scale
    d_normed = total[:, :D]
    mean = jnp.mean(d_normed, axis=1, keepdims=True)
    along = jnp.mean(d_normed * normed, axis=1, keepdims=True)
    d_ref[...] = scale * (d_normed - mean - normed * along)
    diagonal = lax.broadcasted_iota(I32, (4, 4), 0) == lax.broadcasted_iota(I32, (4, 4), 1)
    loss_ref[...] = jnp.sum(
        jnp.where(diagonal, total[:, D : D + 1], 0.0), axis=0, keepdims=True
    )


def effective_of(counts):
    return (1.0 - BETA) / (1.0 - jnp.exp((counts + 1.0) * LOG_BETA))


def label_body(first_ref, digits_ref, labels_ref, target_ref, weight_ref):
    ids = (lax.broadcasted_iota(I32, (1, COLS), 1) + first_ref[0]).astype(F32)
    own = labels_ref[...].astype(F32)
    target = own[:, 0:1] == ids
    for n in range(1, 4):
        target = target | (own[:, n : n + 1] == ids)
    target_ref[...] = jnp.where(target, 1.0, 0.0)
    digits = digits_ref[...].astype(F32)
    labels = digits[:, 0:4] * 256.0 + digits[:, 4:8]
    padded = jnp.concatenate([labels, jnp.zeros((IMAGES, 124), F32)], axis=1)
    turned = jnp.concatenate([padded, jnp.zeros((128 - IMAGES, 128), F32)], axis=0).T
    columns = [labels[:, n : n + 1] for n in range(4)]
    rows = [turned[n : n + 1, :IMAGES] for n in range(4)]

    def fresh_of(entries):
        out = [jnp.ones_like(entries[0])]
        for n in range(1, 4):
            keep = out[0]
            for m in range(n):
                keep = jnp.where(entries[m] == entries[n], 0.0, keep)
            out.append(keep)
        return out

    fresh, fresh_row = fresh_of(columns), fresh_of(rows)
    counts = jnp.zeros((IMAGES, COLS), F32)
    excess = jnp.zeros((IMAGES, 1), F32)
    base = effective_of(jnp.zeros((IMAGES, 1), F32))
    for n in range(4):
        counts = counts + jnp.where(columns[n] == ids, fresh[n], 0.0)
        same = jnp.zeros((IMAGES, IMAGES), F32)
        for m in range(4):
            same = same + jnp.where(columns[n] == rows[m], fresh_row[m], 0.0)
        count = jnp.sum(same, axis=1, keepdims=True)
        excess = excess + fresh[n] * (effective_of(count) - base) / count
    total = CLASSES * base[0:1, :] + jnp.sum(excess, axis=0, keepdims=True)
    weight_ref[...] = effective_of(jnp.sum(counts, axis=0, keepdims=True)) * (CLASSES / total)


def chip_swap(packed):
    dims = packed.shape
    blocks = packed.reshape(CHIPS, CAP // 2, 2, dims[-1])
    return lax.all_to_all(blocks, CHIP, 0, 0, tiled=True).reshape(dims)


def core_swap(rows):
    return lax.ppermute(rows, "core", SWAP)


def shards(tokens, routes, combine, w_in, w_out, out_grad, head_w, labels):
    here = lax.axis_index(Y).astype(I32).reshape(1)
    first_class = (lax.axis_index(EX) * COLS).astype(I32).reshape(1)
    combine = combine.T
    table, x_send = run(
        x_body,
        (shape((2, HALF, TOK), BF16), shape(PACKED_X, BF16)),
        routes.T,
        labels,
        tokens,
        name="dispatch_x",
    )
    x_in = chip_swap(x_send)
    g_send = run(g_body, shape(PACKED, BF16), table, out_grad, combine, name="dispatch_g")
    x_in, g_send = lax.optimization_barrier((x_in, g_send))
    g_in = chip_swap(g_send)
    square = shape(SQUARE, BF16)
    xs, hidden, slope, own, other = expert_kernel(
        forward_body, x_in, core_swap(x_in), (w_in, w_out), (square, square, square, *SENT), "forward"
    )
    other = core_swap(other)
    digits = x_in.reshape(16, 2 * CAP, 2, WIDE)[:, :2, :, D:].reshape(IMAGES, 128)
    targets, class_weight = run(
        label_body,
        (shape((4, COLS), F32), shape((1, COLS), F32)),
        first_class,
        digits,
        labels,
        specs=[SMEM, VMEM, VMEM],
        name="labels",
    )
    g_in, targets, class_weight, mark = lax.optimization_barrier(
        (g_in, targets, class_weight, here)
    )
    mark = run(mark_body, shape((1,), I32), mark, specs=[SMEM], out_specs=SMEM, name="mark", cost=LONG)
    own, mark = lax.optimization_barrier((own, mark))
    out_in = chip_swap(add_cores(own, other, "add_out"))
    own, other, d_w_out, d_w_in = expert_kernel(
        backward_body,
        g_in,
        core_swap(g_in),
        (slope, w_in, w_out, hidden, xs),
        (*SENT, square, square),
        "backward",
    )
    other = core_swap(other)
    mixed_out, d_combine, token_sum = run(
        mixed_body,
        (shape((TOK, D), BF16), shape((2, TOK), F32), shape((1, D), F32)),
        table,
        in_vmem(out_in),
        tokens,
        out_grad,
        combine,
        name="mixed",
        cost=LONG,
    )
    token_sum = lax.psum(token_sum, "core")
    own, token_sum = lax.optimization_barrier((own, token_sum))
    rows_send = add_cores(own, other, "add_rows")
    rows_send, *sums = lax.optimization_barrier((rows_send, *y_parts(token_sum)))
    rows_in = chip_swap(rows_send)
    pooled, part, dp_send = run(
        head_body,
        (shape((4, D), F32), shape((4, D + 128), F32), shape((16, 4, COLS + 128), BF16)),
        here,
        *sums,
        targets,
        class_weight,
        head_w,
        specs=[SMEM] + [VMEM] * 6 + [ANY],
        scratch=[pltpu.VMEM((D, COLS), BF16), pltpu.SemaphoreType.DMA((4,))],
        name="head",
    )
    messages = y_parts(lax.psum(part, "core"))
    d_pooled, losses = run(
        pooled_body,
        (shape((4, D), F32), shape((1, 4), F32)),
        here,
        *messages,
        pooled,
        specs=[SMEM] + [VMEM] * 5,
        name="d_pooled",
    )
    dp_send, rows_in, d_pooled = lax.optimization_barrier((dp_send, rows_in, d_pooled))
    dp_in = lax.all_to_all(dp_send, "dp", 0, 0, tiled=True).reshape(IMAGES, COLS + 128)
    d_tokens = run(tokens_body, shape((TOK, D), BF16), table, in_vmem(rows_in), out_grad, name="d_tokens")
    d_head = dot(dp_in[:, COLS : COLS + 80], dp_in[:, :COLS], 0, 0).astype(BF16)
    return (mixed_out, d_tokens, d_combine.T, d_w_in, d_w_out, losses.reshape(4), d_pooled, d_head)


def solution(mesh):
    grid = Mesh(mesh.devices.reshape(16, 2, 2, 2), ALL)
    rows = P(ALL, None)
    in_specs = (rows, rows, rows, P(None, ALL), rows, rows, P(None, EX), P("dp", None))
    out_specs = (
        rows,
        rows,
        rows,
        P(None, ALL),
        rows,
        P("dp"),
        P("dp", None),
        P("dp", EX),
    )
    return jax.shard_map(shards, mesh=grid, in_specs=in_specs, out_specs=out_specs, check_vma=False)
```
